32 devices in a mesh: blk: 8 (over z, y), hid: 4 (over x, core).
Axes of the slice: x: 2, y: 2, z: 4, core: 2. Of those that a mesh axis runs over, the one named last changes fastest.
Arguments:
- queries: bfloat16 [768, 128], P('blk'), may hold values from -6 to 6
- node_table: bfloat16 [65536, 128], P('blk'), may hold values from -6 to 6
- beam: int32 [768, 128], P('blk'), may hold values from 0 to 65535, as said below
- w_query: bfloat16 [128, 256], P(None, 'hid'), may hold values from -0.5 to 0.5
- w_node: bfloat16 [128, 256], P(None, 'hid'), may hold values from -0.5 to 0.5
- w_cross: bfloat16 [128, 256], P(None, 'hid'), may hold values from -0.5 to 0.5
- bias_hidden: bfloat16 [256], P('hid'), may hold values from -3 to 3
- w_out: bfloat16 [256], P('hid'), may hold values from -0.375 to 0.375
Outputs:
- scores: float32 [768, 128], P('blk', 'hid')
The draws below stay inside these ranges and needn't reach their ends.
Inputs may be any that keep to these rules, and one draw needn't show every extreme that they name: `beam`: each query's entries are distinct and come in sibling pairs 2p, 2p + 1 of 64 parents. Among the rows of one blk index (96 queries) at most 3072 entries lie in any one aligned range of 8192 nodes, and some range holds exactly 3072.
All inputs are finite; a program needn't handle non-finite values.
Results may differ from the reference program's by a relative error of at most 0.007.
Values may be sent and summed in bfloat16 or wider, within the bound.
No kernel may reach another device: no remote copies, remote signals or barrier semaphores. Data moves between devices by JAX's collectives and lax.ppermute only.
A program may use at most 64 MiB of HBM per device.

```python
import math
import jax
import jax.numpy as jnp
from jax import lax

D = 128
HID = 256
BEAM = 128
NODES = 65536
Q_DEV = 96
QUERIES = 768


def draw_beam(key, part):
    groups = QUERIES // Q_DEV
    parent_count = NODES // groups // 2
    per_owner = BEAM // 2 // groups
    most_slots = BEAM // groups
    stride = parent_count // most_slots
    key_hot, key_cold, key_start, key_order = jax.random.split(jax.random.fold_in(key, 17), 4)
    hottest = jax.random.randint(key_hot, (groups,), 0, groups)
    coldest = (hottest + 1 + jax.random.randint(key_cold, (groups,), 0, groups - 1)) % groups
    slots = jnp.arange(BEAM // 2, dtype=jnp.int32)
    base_owner = slots % groups
    base_index = slots // groups
    block_ids = jnp.arange(QUERIES, dtype=jnp.int32) // Q_DEV
    hot_rows = hottest[block_ids][:, None]
    cold_rows = coldest[block_ids][:, None]
    stolen = base_owner[None, :] == cold_rows
    owners = jnp.where(stolen, hot_rows, base_owner[None, :])
    within = jnp.where(stolen, base_index[None, :] + per_owner, base_index[None, :])
    starts = jax.random.randint(key_start, (QUERIES, groups), 0, parent_count)
    chosen = jnp.take_along_axis(starts, owners, axis=1)
    local_parent = (chosen + within * stride) % parent_count
    parents = owners * parent_count + local_parent
    children = jnp.stack([2 * parents, 2 * parents + 1], axis=-1).reshape(QUERIES, BEAM)
    row_keys = jax.random.split(key_order, QUERIES)
    orders = jax.vmap(lambda row_key: jax.random.permutation(row_key, BEAM))(row_keys)
    return jnp.take_along_axis(children, orders, axis=1).astype(jnp.int32)


def block_scale(key, extent, shards, smallest, largest):
    gain, own = 1.0, jax.random.fold_in(key, 6)
    for dim, blocks in shards:
        heights = jnp.exp(jax.random.uniform(jax.random.fold_in(own, dim), (blocks,), jnp.float32, smallest / len(shards), largest / len(shards)))
        gain = gain * jnp.repeat(heights, extent[dim] // blocks).reshape([-1 if axis == dim else 1 for axis in range(len(extent))])
    return gain


def gaussian(key, dims, deviation, reach, cuts=(), held_as=jnp.bfloat16):
    drawn = jax.random.normal(key, dims, jnp.float32) * deviation
    if len(cuts) > 0:
        drawn = block_scale(key, dims, cuts, -0.22, 0.18) * drawn
    return jnp.clip(drawn, min=-reach, max=reach).astype(held_as)


def setup_inputs(seed: int = 0) -> dict:
    streams_of = jax.random.split(jax.random.key(seed), 9)
    queries = gaussian(streams_of[0], (QUERIES, D), 1.0, 6.0, ((0, 8),))
    node_table = gaussian(streams_of[1], (NODES, D), 1.0, 6.0, ((0, 8),))
    beam = draw_beam(jax.random.fold_in(streams_of[8], 71), 0)
    w_query = gaussian(streams_of[3], (D, HID), D ** -0.5, 0.5, ((1, 4),))
    w_node = gaussian(streams_of[4], (D, HID), D ** -0.5, 0.5, ((1, 4),))
    w_cross = gaussian(streams_of[5], (D, HID), D ** -0.5, 0.5, ((1, 4),))
    bias_hidden = gaussian(streams_of[6], (HID,), 0.5, 3.0, ((0, 4),))
    w_out = gaussian(streams_of[7], (HID,), HID ** -0.5, 0.375, ((0, 4),))
    return {"queries": queries, "node_table": node_table, "beam": beam, "w_query": w_query, "w_node": w_node, "w_cross": w_cross, "bias_hidden": bias_hidden, "w_out": w_out}


def reference(queries, node_table, beam, w_query, w_node, w_cross, bias_hidden, w_out):
    block_size = math.gcd(QUERIES, 64)
    query_blocks = queries.reshape(QUERIES // block_size, block_size, D)
    beam_blocks = beam.reshape(QUERIES // block_size, block_size, BEAM)

    def score_block(operands):
        query_rows, beam_rows = operands
        picked = jnp.take(node_table, beam_rows, axis=0)
        cross = (query_rows[:, None, :].astype(jnp.float32) * picked.astype(jnp.float32)).astype(jnp.bfloat16)
        query_part = jnp.dot(query_rows, w_query, preferred_element_type=jnp.float32)
        node_part = jnp.dot(picked.reshape(-1, D), w_node, preferred_element_type=jnp.float32)
        node_part = node_part + jnp.dot(cross.reshape(-1, D), w_cross, preferred_element_type=jnp.float32)
        hidden = node_part.reshape(block_size, BEAM, HID) + query_part[:, None, :] + bias_hidden.astype(jnp.float32)
        hidden = jnp.maximum(hidden, 0.0)
        result = jnp.dot(hidden.reshape(-1, HID), w_out.astype(jnp.float32), precision=lax.Precision.HIGHEST)
        return result.reshape(block_size, BEAM)

    scores = lax.map(score_block, (query_blocks, beam_blocks))
    return scores.reshape(QUERIES, BEAM)
```

```python
import functools

import jax
import jax.numpy as jnp
from jax import lax
from jax.experimental import pallas as pl
from jax.experimental.pallas import tpu as pltpu
from jax.sharding import PartitionSpec as P


SLOT = 8
GROUP = 8
FIELD = 20


def widen_kernel(table_ref, wide_ref):
    wide_ref[...] = table_ref[...].astype(jnp.float32)


def widen(table):
    rows, width = table.shape
    block = min(rows, 1024)
    return pl.pallas_call(
        widen_kernel,
        grid=(rows // block,),
        in_specs=[pl.BlockSpec((block, width), lambda i: (i, 0))],
        out_specs=pl.BlockSpec((block, width), lambda i: (i, 0)),
        out_shape=jax.ShapeDtypeStruct((rows, width), jnp.float32),
        cost_estimate=pl.CostEstimate(flops=0, bytes_accessed=6 * rows * width, transcendentals=0),
    )(table)


def score_kernel(shard_rows, parts, ids_ref, query_ref, table_ref, *refs):
    packs = refs[:parts]
    out_ref, mix_ref, column_ref, start_ref, key_ref, need_ref, flat_ref, total_ref, found_ref, place_ref, done = refs[parts:]
    rows, width = ids_ref.shape
    feat = query_ref.shape[1]
    part = packs[0].shape[1] // 2
    kids = 2 * SLOT
    tile = GROUP * kids

    local = ids_ref[...].astype(jnp.int32) - lax.axis_index("blk") * shard_rows
    owned = (local >= 0) & (local < shard_rows)
    even = owned & ((local & 1) == 0)
    parent = local >> 1
    lane = lax.broadcasted_iota(jnp.int32, (rows, width), 1)
    earlier = (
        lax.broadcasted_iota(jnp.int32, (width, width), 0)
        < lax.broadcasted_iota(jnp.int32, (width, width), 1)
    ).astype(jnp.bfloat16)
    even_count = even.astype(jnp.float32)
    rank = jnp.dot(even_count.astype(jnp.bfloat16), earlier, preferred_element_type=jnp.float32)
    shift = lane - rank.astype(jnp.int32)
    word = jnp.where(even, parent + (shift << FIELD) + (1 << (FIELD + 8)), 0)
    hop = 1
    while hop < width:
        bit = hop << FIELD
        moved = pltpu.roll(word, width - hop, 1)
        word = jnp.where((moved & bit) != 0, moved, jnp.where((word & bit) != 0, 0, word))
        hop *= 2
    front = word & ((1 << FIELD) - 1)
    flat_ref[...] = front * 2
    fetch = pltpu.make_async_copy(flat_ref, place_ref, done)
    fetch.start()
    need_ref[...] = jnp.where(word != 0, front, -1)
    key_ref[...] = jnp.where(owned, local, -4)
    most = jnp.max(jnp.sum(even_count, axis=1, keepdims=True)).astype(jnp.int32)
    passes = (most + (SLOT - 1)) // SLOT

    mix_ref[0:feat, :] = jnp.concatenate([p[0:feat, part:] for p in packs], axis=1)
    mix_ref[feat:, :] = jnp.concatenate([p[feat:, 0:part] for p in packs], axis=1)
    half = jnp.concatenate([p[feat : feat + part, part:] for p in packs], axis=0)
    column_ref[...] = jnp.concatenate([half] * (width // part), axis=1)
    query_weights = jnp.concatenate([p[0:feat, 0:part] for p in packs], axis=1)
    bias = jnp.concatenate([p[feat + part : feat + part + 1, part:] for p in packs], axis=1)
    start_ref[...] = jnp.dot(
        query_ref[...], query_weights, preferred_element_type=jnp.float32
    ) + bias.astype(jnp.float32)
    total_ref[...] = jnp.zeros((rows, width), jnp.float32)
    fetch.wait()

    def one_pass(c, carry):
        def gather(g, inner):
            for i in range(GROUP):
                for t in range(SLOT):
                    at = pl.multiple_of(place_ref[g * GROUP + i, c * SLOT + t], 2)
                    to = pl.multiple_of(g * tile, tile) + (i * kids + 2 * t)
                    found_ref[pl.ds(to, 2), :] = table_ref[pl.ds(at, 2), :]
            return inner

        lax.fori_loop(0, rows // GROUP, gather, 0)

        def score(g, inner):
            some = pl.ds(pl.multiple_of(g * GROUP, GROUP), GROUP)
            nodes = found_ref[pl.ds(pl.multiple_of(g * tile, tile), tile), :]
            query = query_ref[some, :].astype(jnp.float32)
            spread = jnp.broadcast_to(query[:, None, :], (GROUP, kids, feat)).reshape(tile, feat)
            joined = jnp.concatenate(
                [nodes.astype(jnp.bfloat16), (nodes * spread).astype(jnp.bfloat16)], axis=1
            )
            pre = jnp.dot(joined, mix_ref[...], preferred_element_type=jnp.float32)
            hidden_width = pre.shape[1]
            begin = start_ref[some, :]
            hidden = jnp.maximum(pre.reshape(GROUP, kids, hidden_width) + begin[:, None, :], 0.0)
            hidden = hidden.reshape(tile, hidden_width).astype(jnp.bfloat16)
            score = jnp.dot(hidden, column_ref[...], preferred_element_type=jnp.float32)
            need = pltpu.roll(need_ref[some, :], (width - c * SLOT) % width, 1)
            key = key_ref[some, :]
            above = key >> 1
            parity = key & 1
            code = jnp.full((GROUP, width), -1, jnp.int32)
            for t in range(SLOT):
                code = jnp.where(above == need[:, t : t + 1], 2 * t + parity, code)
            slot = lax.broadcasted_iota(jnp.int32, (GROUP, kids, width), 1)
            hit = code[:, None, :] == slot
            total_ref[some, :] += jnp.sum(
                jnp.where(hit, score.reshape(GROUP, kids, width), 0.0), axis=1
            )
            return inner

        lax.fori_loop(0, rows // GROUP, score, 0)
        return carry

    lax.fori_loop(0, passes, one_pass, 0)
    out_ref[...] = total_ref[...].astype(out_ref.dtype)


def score_source(ids, queries, wide, packs, shard_rows):
    rows, width = ids.shape
    feat = queries.shape[1]
    hidden = len(packs) * packs[0].shape[1] // 2
    slots = rows * 2 * SLOT
    vmem = pl.BlockSpec(memory_space=pltpu.VMEM)
    return pl.pallas_call(
        functools.partial(score_kernel, shard_rows, len(packs)),
        in_specs=[vmem] * (3 + len(packs)),
        out_specs=vmem,
        out_shape=jax.ShapeDtypeStruct((rows, width), jnp.bfloat16),
        scratch_shapes=[
            pltpu.VMEM((2 * feat, hidden), jnp.bfloat16),
            pltpu.VMEM((hidden, width), jnp.bfloat16),
            pltpu.VMEM((rows, hidden), jnp.float32),
            pltpu.VMEM((rows, width), jnp.int32),
            pltpu.VMEM((rows, width), jnp.int32),
            pltpu.VMEM((rows, width), jnp.int32),
            pltpu.VMEM((rows, width), jnp.float32),
            pltpu.VMEM((slots, feat), jnp.float32),
            pltpu.SMEM((rows, width), jnp.int32),
            pltpu.SemaphoreType.DMA,
        ],
        cost_estimate=pl.CostEstimate(
            flops=2 * slots * 3 * feat * hidden, bytes_accessed=4 * slots * feat, transcendentals=0
        ),
    )(ids, queries, wide, *packs)


def mirrored(value, count):
    result = 0
    while count > 1:
        result = result * 2 + value % 2
        value //= 2
        count //= 2
    return result


def shards(queries, node_table, beam, w_query, w_node, w_cross, bias_hidden, w_out):
    groups = lax.axis_size("blk")
    parts = lax.axis_size("hid")
    rows, width = beam.shape
    feat, part = w_query.shape
    shard_rows = node_table.shape[0]
    binary = groups & (groups - 1) == 0 and parts & (parts - 1) == 0
    turns = groups // parts

    def hop_pairs(turn, back):
        pairs = []
        for b in range(groups):
            for h in range(parts):
                k = (mirrored(h, parts) if binary else h) * turns + turn
                if binary:
                    to = b ^ k
                else:
                    to = (b - k) % groups if not back else (b + k) % groups
                pairs.append((b * parts + h, to * parts + h))
        return pairs

    def hop(value, turn, back=False):
        return lax.ppermute(value, ("blk", "hid"), hop_pairs(turn, back))

    def across(value, step):
        pairs = [(h, h ^ step if binary else (h + step) % parts) for h in range(parts)]
        return lax.ppermute(value, "hid", pairs)

    short = jnp.uint16 if groups * shard_rows <= 65536 else jnp.int32
    ids = beam.astype(short)
    asked = [(hop(ids, turn), hop(queries, turn)) for turn in range(turns)]

    side = jnp.concatenate(
        [
            jnp.broadcast_to(w_out[:, None], (part, part)),
            bias_hidden[None, :],
            jnp.zeros((feat - part - 1, part), w_out.dtype),
        ],
        axis=0,
    )
    pack = jnp.concatenate(
        [
            jnp.concatenate([w_query, w_node], axis=1),
            jnp.concatenate([w_cross, side], axis=1),
        ],
        axis=0,
    )
    packs = [pack] + [across(pack, step) for step in range(1, parts)]
    wide = widen(node_table)

    total = None
    for turn, (source_ids, source_queries) in enumerate(asked):
        scored = score_source(source_ids, source_queries, wide, packs, shard_rows)
        back = hop(scored, turn, True).astype(jnp.float32)
        total = back if total is None else total + back

    own = lax.axis_index("hid")
    piece = width // parts
    result = lax.dynamic_slice_in_dim(total, own * piece, piece, axis=1)
    for step in range(1, parts):
        peer = own ^ step if binary else (own + step) % parts
        sent = lax.dynamic_slice_in_dim(total, peer * piece, piece, axis=1)
        result = result + across(sent.astype(jnp.bfloat16), step).astype(jnp.float32)
    return result


def solution(mesh):
    in_specs = (
        P("blk", None),
        P("blk", None),
        P("blk", None),
        P(None, "hid"),
        P(None, "hid"),
        P(None, "hid"),
        P("hid"),
        P("hid"),
    )
    out_specs = P("blk", "hid")
    return jax.shard_map(shards, mesh=mesh, in_specs=in_specs, out_specs=out_specs, check_vma=False)
```

```python
import functools

import jax
import jax.numpy as jnp
from jax import lax
from jax.experimental import pallas as pl
from jax.experimental.pallas import tpu as pltpu
from jax.sharding import PartitionSpec as P


SLOT = 8
KIDS = 2 * SLOT
GROUP = 8
FIELD = 20
DIGIT = 256

VMEM = pl.BlockSpec(memory_space=pltpu.VMEM)


def rows_by_rows(left, right):
    return lax.dot_general(
        left, right, (((1,), (1,)), ((), ())), preferred_element_type=jnp.float32
    )


def prepare_kernel(part, table_ref, *refs):
    packs = refs[:-4]
    wide_ref, mix_ref, first_ref, column_ref = refs[-4:]
    feat = table_ref.shape[1]

    @pl.when(pl.program_id(0) == 0)
    def _():
        stacked = [
            jnp.concatenate([p[i * part : (i + 1) * part, :] for p in packs], axis=0)
            for i in range(4)
        ]
        first_ref[0:feat, :] = stacked[0].T
        mix_ref[0:feat, :] = stacked[1].T
        mix_ref[feat:, :] = stacked[2].T
        last = stacked[3]
        column_ref[...] = jnp.broadcast_to(last[:, 0:1], column_ref.shape)
        first_ref[feat:, :] = last.T

    wide_ref[...] = table_ref[...].astype(jnp.float32)


def prepare(table, packs):
    rows, width = table.shape
    block = min(rows, 2048)
    part = packs[0].shape[0] // 4
    hidden = part * len(packs)
    whole = lambda shape: pl.BlockSpec(shape, lambda i: (0, 0))
    return pl.pallas_call(
        functools.partial(prepare_kernel, part),
        grid=(rows // block,),
        in_specs=[pl.BlockSpec((block, width), lambda i: (i, 0))]
        + [whole(packs[0].shape)] * len(packs),
        out_specs=(
            pl.BlockSpec((block, width), lambda i: (i, 0)),
            whole((2 * width, hidden)),
            whole((2 * width, hidden)),
            whole((hidden, width)),
        ),
        out_shape=(
            jax.ShapeDtypeStruct((rows, width), jnp.float32),
            jax.ShapeDtypeStruct((2 * width, hidden), jnp.bfloat16),
            jax.ShapeDtypeStruct((2 * width, hidden), jnp.bfloat16),
            jax.ShapeDtypeStruct((hidden, width), jnp.bfloat16),
        ),
        compiler_params=pltpu.CompilerParams(vmem_limit_bytes=12 * 2**20),
        cost_estimate=pl.CostEstimate(flops=0, bytes_accessed=6 * rows * width, transcendentals=0),
    )(table, *packs)


def score_kernel(
    shard_rows,
    digits,
    tile_queries,
    asked_ref,
    table_ref,
    mix_ref,
    first_ref,
    column_ref,
    out_ref,
    start_ref,
    key_ref,
    need_ref,
    flat_ref,
    total_ref,
    found_ref,
    place_ref,
    done,
):
    rows, width = key_ref.shape
    feat = table_ref.shape[1]
    hidden_width = mix_ref.shape[1]
    group_rows = GROUP * KIDS
    tile = tile_queries * KIDS

    ids = asked_ref[rows : 2 * rows, :].astype(jnp.int32)
    for d in range(1, digits):
        ids = ids * DIGIT + asked_ref[(d + 1) * rows : (d + 2) * rows, :].astype(jnp.int32)
    local = ids - lax.axis_index("blk") * shard_rows
    owned = (local >= 0) & (local < shard_rows)
    even = owned & ((local & 1) == 0)
    parent = local >> 1
    lane = lax.broadcasted_iota(jnp.int32, (rows, width), 1)
    earlier = (
        lax.broadcasted_iota(jnp.int32, (width, width), 0)
        < lax.broadcasted_iota(jnp.int32, (width, width), 1)
    ).astype(jnp.bfloat16)
    even_count = even.astype(jnp.float32)
    rank = jnp.dot(even_count.astype(jnp.bfloat16), earlier, preferred_element_type=jnp.float32)
    shift = lane - rank.astype(jnp.int32)
    word = jnp.where(even, parent + (shift << FIELD) + (1 << (FIELD + 8)), 0)
    hop = 1
    while hop < width:
        bit = hop << FIELD
        moved = pltpu.roll(word, width - hop, 1)
        word = jnp.where((moved & bit) != 0, moved, jnp.where((word & bit) != 0, 0, word))
        hop *= 2
    front = word & ((1 << FIELD) - 1)
    flat_ref[...] = front * 2
    fetch = pltpu.make_async_copy(flat_ref, place_ref, done)
    fetch.start()
    need_ref[...] = jnp.where(word != 0, front, -1)
    key_ref[...] = jnp.where(owned, local, -4)
    most = jnp.max(jnp.sum(even_count, axis=1, keepdims=True)).astype(jnp.int32)
    passes = (most + (SLOT - 1)) // SLOT

    pick = (lax.broadcasted_iota(jnp.int32, (rows, feat), 1) == feat // 2).astype(jnp.bfloat16)
    query_and_one = jnp.concatenate([asked_ref[0:rows, :], pick], axis=1)
    start_ref[...] = jnp.dot(query_and_one, first_ref[...], preferred_element_type=jnp.float32)
    total_ref[...] = jnp.zeros((rows, width), jnp.float32)
    fetch.wait()

    def one_pass(c):
        def gather(g, inner):
            for i in range(GROUP):
                for t in range(SLOT):
                    at = pl.multiple_of(place_ref[g * GROUP + i, c * SLOT + t], 2)
                    to = pl.multiple_of(g * group_rows, group_rows) + (i * KIDS + 2 * t)
                    found_ref[pl.ds(to, 2), :] = table_ref[pl.ds(at, 2), :]
            return inner

        lax.fori_loop(0, rows // GROUP, gather, 0)

        def score(g, inner):
            some = pl.ds(pl.multiple_of(g * tile_queries, tile_queries), tile_queries)
            nodes = found_ref[pl.ds(pl.multiple_of(g * tile, tile), tile), :]
            query = asked_ref[some, :].astype(jnp.float32)
            spread = jnp.broadcast_to(query[:, None, :], (tile_queries, KIDS, feat))
            crossed = (nodes * spread.reshape(tile, feat)).astype(jnp.bfloat16)
            joined = jnp.concatenate([nodes.astype(jnp.bfloat16), crossed], axis=1)
            pre = jnp.dot(joined, mix_ref[...], preferred_element_type=jnp.float32)
            begin = start_ref[some, :]
            hidden = pre.reshape(tile_queries, KIDS, hidden_width) + begin[:, None, :]
            hidden = jnp.maximum(hidden, 0.0).reshape(tile, hidden_width).astype(jnp.bfloat16)
            score = jnp.dot(hidden, column_ref[...], preferred_element_type=jnp.float32)
            need = need_ref[some, :]
            if not isinstance(c, int) or c > 0:
                need = pltpu.roll(need, (width - c * SLOT) % width, 1)
            key = key_ref[some, :]
            above = key >> 1
            parity = key & 1
            code = jnp.full((tile_queries, width), -1, jnp.int32)
            for t in range(SLOT):
                code = jnp.where(above == need[:, t : t + 1], 2 * t + parity, code)
            slot = lax.broadcasted_iota(jnp.int32, (tile_queries, KIDS, width), 1)
            hit = code[:, None, :] == slot
            total_ref[some, :] += jnp.sum(
                jnp.where(hit, score.reshape(tile_queries, KIDS, width), 0.0), axis=1
            )
            return inner

        lax.fori_loop(0, rows // tile_queries, score, 0)

    pl.when(passes > 0)(lambda: one_pass(0))
    pl.when(passes > 1)(lambda: one_pass(1))

    def later(c, inner):
        one_pass(c)
        return inner

    lax.fori_loop(2, passes, later, 0)
    out_ref[...] = total_ref[...].T.astype(out_ref.dtype)


def score_source(asked, rows, shard_rows, wide, mix, first, column):
    feat = asked.shape[1]
    digits = asked.shape[0] // rows - 1
    hidden, width = column.shape
    slots = rows * KIDS
    tile_queries = next(n for n in (32, 24, 16, 8) if rows % n == 0)
    return pl.pallas_call(
        functools.partial(score_kernel, shard_rows, digits, tile_queries),
        in_specs=[VMEM] * 5,
        out_specs=VMEM,
        out_shape=jax.ShapeDtypeStruct((width, rows), jnp.bfloat16),
        scratch_shapes=[
            pltpu.VMEM((rows, hidden), jnp.float32),
            pltpu.VMEM((rows, width), jnp.int32),
            pltpu.VMEM((rows, width), jnp.int32),
            pltpu.VMEM((rows, width), jnp.int32),
            pltpu.VMEM((rows, width), jnp.float32),
            pltpu.VMEM((slots, feat), jnp.float32),
            pltpu.SMEM((rows, width), jnp.int32),
            pltpu.SemaphoreType.DMA,
        ],
        compiler_params=pltpu.CompilerParams(vmem_limit_bytes=16 * 2**20),
        cost_estimate=pl.CostEstimate(
            flops=2 * slots * 3 * feat * hidden, bytes_accessed=4 * slots * feat, transcendentals=0
        ),
    )(asked, wide, mix, first, column)


def mirrored(value, count):
    result = 0
    while count > 1:
        result = result * 2 + value % 2
        value //= 2
        count //= 2
    return result


def shards(queries, node_table, beam, w_query, w_node, w_cross, bias_hidden, w_out):
    groups = lax.axis_size("blk")
    parts = lax.axis_size("hid")
    rows, width = beam.shape
    feat, part = w_query.shape
    shard_rows = node_table.shape[0]
    binary = groups & (groups - 1) == 0 and parts & (parts - 1) == 0
    turns = groups // parts

    def hop_pairs(turn, back):
        pairs = []
        for b in range(groups):
            for h in range(parts):
                k = (mirrored(h, parts) if binary else h) * turns + turn
                if binary:
                    to = b ^ k
                else:
                    to = (b - k) % groups if not back else (b + k) % groups
                pairs.append((b * parts + h, to * parts + h))
        return pairs

    def hop(value, turn, back=False):
        return lax.ppermute(value, ("blk", "hid"), hop_pairs(turn, back))

    def across(value, step):
        pairs = [(h, h ^ step if binary else (h + step) % parts) for h in range(parts)]
        return lax.ppermute(value, "hid", pairs)

    digits = []
    left = groups * shard_rows - 1
    rest = beam
    while left > 0:
        digits.insert(0, (rest % DIGIT).astype(queries.dtype))
        rest = rest // DIGIT
        left //= DIGIT
    message = jnp.concatenate([queries] + digits, axis=0)
    asked = [hop(message, turn) for turn in range(turns)]

    half = jnp.arange(feat, dtype=jnp.int32)[None, :] < feat // 2
    last = jnp.where(half, w_out[:, None], bias_hidden[:, None])
    pack = jnp.concatenate([w_query.T, w_node.T, w_cross.T, last], axis=0)
    packs = [pack] + [across(pack, step) for step in range(1, parts)]
    prepared = prepare(node_table, packs)

    total = None
    for turn in range(turns):
        scored = score_source(asked[turn], rows, shard_rows, *prepared)
        back = hop(scored, turn, True).astype(jnp.float32)
        total = back if total is None else total + back

    own = lax.axis_index("hid")
    piece = width // parts
    result = lax.dynamic_slice_in_dim(total, own * piece, piece, axis=0)
    for step in range(1, parts):
        peer = own ^ step if binary else (own + step) % parts
        sent = lax.dynamic_slice_in_dim(total, peer * piece, piece, axis=0)
        result = result + across(sent.astype(jnp.bfloat16), step).astype(jnp.float32)
    return result.T


def solution(mesh):
    in_specs = (
        P("blk", None),
        P("blk", None),
        P("blk", None),
        P(None, "hid"),
        P(None, "hid"),
        P(None, "hid"),
        P("hid"),
        P("hid"),
    )
    out_specs = P("blk", "hid")
    return jax.shard_map(shards, mesh=mesh, in_specs=in_specs, out_specs=out_specs, check_vma=False)
```

```python
import functools

import jax
import jax.numpy as jnp
from jax import lax
from jax.experimental import pallas as pl
from jax.experimental.pallas import tpu as pltpu
from jax.sharding import PartitionSpec as P


SLOT = 8
KIDS = 2 * SLOT
READY = 2
FIELD = 20
SHIFT = 8
LANES = 128

VMEM = pl.BlockSpec(memory_space=pltpu.VMEM)


def pack_kernel(digits, *refs):
    sources, (message_ref, pack_ref), held, done = refs[:7], refs[7:9], refs[9:-1], refs[-1]
    copies = [
        pltpu.make_async_copy(source, target, done.at[i])
        for i, (source, target) in enumerate(zip(sources, held))
    ]
    for copy in copies:
        copy.start()
    beam_ref, query_ref = held[:2]
    weights, (out_row, bias_row) = held[2:5], held[5:7]
    rows = beam_ref.shape[0]
    part = weights[0].shape[0]
    width = pack_ref.shape[1]
    for copy in copies:
        copy.wait()
    ids = beam_ref[...]
    for d in range(digits):
        digit = (ids >> (SHIFT * (digits - 1 - d))) & (2**SHIFT - 1)
        message_ref[(d + 1) * rows : (d + 2) * rows, :] = digit.astype(jnp.float32).astype(
            jnp.bfloat16
        )
    message_ref[0:rows, :] = query_ref[...]
    for i, weight in enumerate(weights):
        pack_ref[i * part : (i + 1) * part, :] = weight[...]
    tail = pack_ref.shape[0] - 3 * part
    ends = jnp.concatenate(
        [
            out_row[...].astype(jnp.float32),
            bias_row[...].astype(jnp.float32),
            jnp.zeros((tail - 2, part), jnp.float32),
        ],
        axis=0,
    )
    ends = jnp.concatenate([ends, jnp.zeros((tail, width - part), jnp.float32)], axis=1)
    pack_ref[3 * part :, :] = ends.astype(jnp.bfloat16)


def pack(queries, beam, digits, weights, w_out, bias):
    rows, width = queries.shape
    part = w_out.shape[0]
    given = (beam, queries, *[w.T for w in weights], w_out[None, :], bias[None, :])
    return pl.pallas_call(
        functools.partial(pack_kernel, digits),
        in_specs=[pl.BlockSpec(memory_space=pltpu.HBM)] * len(given),
        out_specs=(VMEM, VMEM),
        out_shape=(
            jax.ShapeDtypeStruct(((digits + 1) * rows, width), jnp.bfloat16),
            jax.ShapeDtypeStruct((3 * part + 16, width), jnp.bfloat16),
        ),
        scratch_shapes=[pltpu.VMEM(x.shape, x.dtype) for x in given]
        + [pltpu.SemaphoreType.DMA((len(given),))],
        compiler_params=pltpu.CompilerParams(vmem_limit_bytes=60 * 2**20),
    )(*given)


def widen_kernel(chunks, table_ref, wide_ref, held_ref, done):
    rows = table_ref.shape[0] // chunks
    copies = [
        pltpu.make_async_copy(
            table_ref.at[pl.ds(i * rows, rows)], held_ref.at[pl.ds(i * rows, rows)], done.at[i]
        )
        for i in range(chunks)
    ]
    for copy in copies:
        copy.start()
    for i, copy in enumerate(copies):
        copy.wait()
        some = slice(i * rows, (i + 1) * rows)
        wide_ref[some, :] = held_ref[some, :].astype(jnp.float32)


def widen(table):
    rows, width = table.shape
    chunks = 8
    return pl.pallas_call(
        functools.partial(widen_kernel, chunks),
        in_specs=[pl.BlockSpec(memory_space=pltpu.HBM)],
        out_specs=VMEM,
        out_shape=jax.ShapeDtypeStruct((rows, width), jnp.float32),
        scratch_shapes=[pltpu.VMEM((rows, width), table.dtype), pltpu.SemaphoreType.DMA((chunks,))],
        compiler_params=pltpu.CompilerParams(vmem_limit_bytes=12 * 2**20),
        cost_estimate=pl.CostEstimate(flops=0, bytes_accessed=6 * rows * width, transcendentals=0),
    )(table)


def score_kernel(shard_rows, digits, turns, parts, tile_queries, *refs):
    asked, table_ref, packs = refs[:turns], refs[turns], refs[turns + 1 : turns + 1 + parts]
    outs = refs[turns + 1 + parts : 2 * turns + 1 + parts]
    (
        mix_ref,
        column_ref,
        sum_ref,
        query_ref,
        start_ref,
        key_ref,
        need_ref,
        flat_ref,
        total_ref,
        found_ref,
        place_ref,
        passes_ref,
        done,
    ) = refs[2 * turns + 1 + parts :]
    width, rows = outs[0].shape
    feat = table_ref.shape[1]
    hidden_width = mix_ref.shape[1]
    part = hidden_width // parts
    tile = tile_queries * KIDS
    tiles = rows // tile_queries
    limit = width // 2 // SLOT

    ids = jnp.concatenate([a[rows : 2 * rows, :] for a in asked], axis=0).astype(jnp.int32)
    for d in range(2, digits + 1):
        digit = jnp.concatenate([a[d * rows : (d + 1) * rows, :] for a in asked], axis=0)
        ids = (ids << SHIFT) + digit.astype(jnp.int32)
    local = ids - lax.axis_index("blk") * shard_rows
    owned = (local >= 0) & (local < shard_rows)
    even = owned & ((local & 1) == 0)
    lane = lax.broadcasted_iota(jnp.int32, (turns * rows, width), 1)
    earlier = (
        lax.broadcasted_iota(jnp.int32, (width, width), 0)
        < lax.broadcasted_iota(jnp.int32, (width, width), 1)
    ).astype(jnp.bfloat16)
    even_count = even.astype(jnp.float32)
    rank = jnp.dot(even_count.astype(jnp.bfloat16), earlier, preferred_element_type=jnp.float32)
    shift = lane - rank.astype(jnp.int32)
    word = jnp.where(even, (local >> 1) + (shift << FIELD) + (1 << (FIELD + 8)), 0)
    hop = 1
    while hop < width:
        bit = hop << FIELD
        moved = pltpu.roll(word, width - hop, 1)
        word = jnp.where((moved & bit) != 0, moved, jnp.where((word & bit) != 0, 0, word))
        hop *= 2
    front = word & ((1 << FIELD) - 1)
    ahead = []
    for j in range(turns):
        slots = (front[j * rows : (j + 1) * rows, :] * 2).T
        for c in range(limit):
            flat_ref[j * limit + c, :, 0:rows] = slots[c * SLOT : (c + 1) * SLOT, :]
        ahead.append(
            pltpu.make_async_copy(
                flat_ref.at[pl.ds(j * limit, READY)],
                place_ref.at[pl.ds(j * READY, READY)],
                done.at[j],
            )
        )
        ahead[-1].start()
        most = jnp.max(
            jnp.sum(even_count[j * rows : (j + 1) * rows, :], axis=1, keepdims=True)
        ).astype(jnp.int32)
        passes_ref[j] = (most + (SLOT - 1)) // SLOT
    need_ref[...] = jnp.where(word != 0, front, -1)
    key_ref[...] = jnp.where(owned, local, -4)

    stacked = [
        jnp.concatenate([p[i * part : (i + 1) * part, :] for p in packs], axis=0) for i in range(3)
    ]
    mix_ref[0:feat, :] = stacked[1].T
    mix_ref[feat:, :] = stacked[2].T
    ends = [p[3 * part :, :].astype(jnp.float32) for p in packs]
    out_row = jnp.concatenate([e[0:1, 0:part] for e in ends], axis=1)
    bias = jnp.concatenate([e[1:2, 0:part] for e in ends], axis=1)
    column_ref[...] = jnp.broadcast_to(out_row, (width, hidden_width)).T.astype(jnp.bfloat16)
    queries = jnp.concatenate([a[0:rows, :] for a in asked], axis=0)
    query_ref[...] = queries.astype(jnp.float32)
    start_ref[...] = (
        jnp.dot(queries, stacked[0].T, preferred_element_type=jnp.float32) + bias
    )
    sum_ref[...] = (
        lax.broadcasted_iota(jnp.int32, (tile_queries, tile), 1) // KIDS
        == lax.broadcasted_iota(jnp.int32, (tile_queries, tile), 0)
    ).astype(jnp.bfloat16)
    total_ref[...] = jnp.zeros(total_ref.shape, jnp.float32)
    for copy in ahead:
        copy.wait()

    def gather(block, k):
        for i in range(tile_queries):
            for t in range(SLOT):
                at = pl.multiple_of(place_ref[block, t, k * tile_queries + i], 2)
                found_ref[k, pl.ds(i * KIDS + 2 * t, 2), :] = table_ref[pl.ds(at, 2), :]

    def score(j, c, k):
        first = pl.multiple_of(j * rows + k * tile_queries, tile_queries)
        some = pl.ds(first, tile_queries)
        nodes = found_ref[k]
        spread = jnp.broadcast_to(query_ref[some, :][:, None, :], (tile_queries, KIDS, feat))
        crossed = (nodes * spread.reshape(tile, feat)).astype(jnp.bfloat16)
        joined = jnp.concatenate([nodes.astype(jnp.bfloat16), crossed], axis=1)
        pre = jnp.dot(joined, mix_ref[...], preferred_element_type=jnp.float32)
        pre = pre.reshape(tile_queries, KIDS, hidden_width) + start_ref[some, :][:, None, :]
        hidden = jnp.maximum(pre.reshape(tile, hidden_width).astype(jnp.bfloat16), 0)
        score = jnp.dot(hidden, column_ref[...], preferred_element_type=jnp.float32)
        need = pltpu.roll(need_ref[some, :], (width - c * SLOT) % width, 1)
        key = key_ref[some, :]
        above = key >> 1
        parity = key & 1
        code = jnp.full((tile_queries, width), -1, jnp.int32)
        for t in range(SLOT):
            code = jnp.where(above == need[:, t : t + 1], 2 * t + parity, code)
        slot = lax.broadcasted_iota(jnp.int32, (tile_queries, KIDS, width), 1)
        hit = code[:, None, :] == slot
        hits = jnp.where(hit, score.reshape(tile_queries, KIDS, width), 0.0)
        total_ref[some, :] += jnp.dot(
            sum_ref[...],
            hits.reshape(tile, width).astype(jnp.bfloat16),
            preferred_element_type=jnp.float32,
        )

    def one_source(j, carry):
        def one_pass(c, inner):
            @pl.when(c >= READY)
            def _():
                copy = pltpu.make_async_copy(
                    flat_ref.at[j * limit + c], place_ref.at[turns * READY], done.at[turns]
                )
                copy.start()
                copy.wait()

            block = jnp.where(c < READY, j * READY + c, turns * READY)
            gather(block, 0)
            for k in range(tiles):
                if k + 1 < tiles:
                    gather(block, k + 1)
                score(j, c, k)
            return inner

        return lax.fori_loop(0, passes_ref[j], one_pass, carry)

    lax.fori_loop(0, turns, one_source, 0)
    for j, out_ref in enumerate(outs):
        out_ref[...] = total_ref[j * rows : (j + 1) * rows, :].T.astype(out_ref.dtype)


def score_sources(asked, rows, shard_rows, wide, packs):
    turns = len(asked)
    feat = asked[0].shape[1]
    width = feat
    digits = asked[0].shape[0] // rows - 1
    part = (packs[0].shape[0] - 16) // 3
    hidden = part * len(packs)
    tile_queries = next(n for n in (32, 24, 16, 8) if rows % n == 0)
    tile = tile_queries * KIDS
    lanes = -(-rows // LANES) * LANES
    count = turns * rows
    return pl.pallas_call(
        functools.partial(score_kernel, shard_rows, digits, turns, len(packs), tile_queries),
        in_specs=[VMEM] * (turns + 1 + len(packs)),
        out_specs=(VMEM,) * turns,
        out_shape=(jax.ShapeDtypeStruct((width, rows), jnp.bfloat16),) * turns,
        scratch_shapes=[
            pltpu.VMEM((2 * feat, hidden), jnp.bfloat16),
            pltpu.VMEM((hidden, width), jnp.bfloat16),
            pltpu.VMEM((tile_queries, tile), jnp.bfloat16),
            pltpu.VMEM((count, feat), jnp.float32),
            pltpu.VMEM((count, hidden), jnp.float32),
            pltpu.VMEM((count, width), jnp.int32),
            pltpu.VMEM((count, width), jnp.int32),
            pltpu.VMEM((turns * (width // 2 // SLOT), SLOT, lanes), jnp.int32),
            pltpu.VMEM((count, width), jnp.float32),
            pltpu.VMEM((rows // tile_queries, tile, feat), jnp.float32),
            pltpu.SMEM((turns * READY + 1, SLOT, lanes), jnp.int32),
            pltpu.SMEM((turns,), jnp.int32),
            pltpu.SemaphoreType.DMA((turns + 1,)),
        ],
        compiler_params=pltpu.CompilerParams(vmem_limit_bytes=16 * 2**20),
        cost_estimate=pl.CostEstimate(
            flops=2 * count * KIDS * 3 * feat * hidden,
            bytes_accessed=4 * count * KIDS * feat,
            transcendentals=0,
        ),
    )(*asked, wide, *packs)


def mirrored(value, count):
    result = 0
    while count > 1:
        result = result * 2 + value % 2
        value //= 2
        count //= 2
    return result


def shards(queries, node_table, beam, w_query, w_node, w_cross, bias_hidden, w_out):
    groups = lax.axis_size("blk")
    parts = lax.axis_size("hid")
    rows, width = beam.shape
    shard_rows = node_table.shape[0]
    binary = groups & (groups - 1) == 0 and parts & (parts - 1) == 0
    turns = groups // parts

    def hop_pairs(turn, back):
        pairs = []
        for b in range(groups):
            for h in range(parts):
                k = (mirrored(h, parts) if binary else h) * turns + turn
                if binary:
                    to = b ^ k
                else:
                    to = (b - k) % groups if not back else (b + k) % groups
                pairs.append((b * parts + h, to * parts + h))
        return pairs

    def hop(value, turn, back=False):
        return lax.ppermute(value, ("blk", "hid"), hop_pairs(turn, back))

    def across(value, step):
        pairs = [(h, h ^ step if binary else (h + step) % parts) for h in range(parts)]
        return lax.ppermute(value, "hid", pairs)

    digits = -(-(groups * shard_rows - 1).bit_length() // SHIFT)
    message, weights = pack(queries, beam, digits, (w_query, w_node, w_cross), w_out, bias_hidden)
    asked = [hop(message, turn) for turn in range(turns)]
    packs = [weights] + [across(weights, step) for step in range(1, parts)]
    scored = score_sources(asked, rows, shard_rows, widen(node_table), packs)
    total = sum(hop(s, turn, True).astype(jnp.float32) for turn, s in enumerate(scored))

    own = lax.axis_index("hid")
    piece = width // parts
    result = lax.dynamic_slice_in_dim(total, own * piece, piece, axis=0)
    for step in range(1, parts):
        peer = own ^ step if binary else (own + step) % parts
        sent = lax.dynamic_slice_in_dim(total, peer * piece, piece, axis=0)
        result = result + across(sent.astype(jnp.bfloat16), step).astype(jnp.float32)
    return result.T


def solution(mesh):
    in_specs = (
        P("blk", None),
        P("blk", None),
        P("blk", None),
        P(None, "hid"),
        P(None, "hid"),
        P(None, "hid"),
        P("hid"),
        P("hid"),
    )
    out_specs = P("blk", "hid")
    return jax.shard_map(shards, mesh=mesh, in_specs=in_specs, out_specs=out_specs, check_vma=False)
```

```python
import functools

import jax
import jax.numpy as jnp
from jax import lax
from jax.experimental import pallas as pl
from jax.experimental.pallas import tpu as pltpu
from jax.sharding import PartitionSpec as P


SLOT = 8
KIDS = 2 * SLOT
READY = 2
FIELD = 20
SHIFT = 8
LANES = 128
SUBLANES = 8
TAIL = 16

VMEM = pl.BlockSpec(memory_space=pltpu.VMEM)


def prepare_kernel(part, table_ref, *refs):
    packs = refs[:-5]
    wide_ref, mix_ref, first_ref, column_ref, bias_ref = refs[-5:]
    feat = table_ref.shape[1]

    @pl.when(pl.program_id(0) == 0)
    def _():
        stacked = [
            jnp.concatenate([p[i * part : (i + 1) * part, :] for p in packs], axis=0)
            for i in range(3)
        ]
        first_ref[...] = stacked[0].T
        mix_ref[0:feat, :] = stacked[1].T
        mix_ref[feat:, :] = stacked[2].T
        ends = [p[3 * part :, :].astype(jnp.float32) for p in packs]
        out_row = jnp.concatenate([e[0:1, 0:part] for e in ends], axis=1)
        bias = jnp.concatenate([e[1:2, 0:part] for e in ends], axis=1)
        column_ref[...] = (
            jnp.broadcast_to(out_row, (feat, out_row.shape[1])).T.astype(jnp.bfloat16)
        )
        bias_ref[...] = jnp.broadcast_to(bias, bias_ref.shape)

    wide_ref[...] = table_ref[...].astype(jnp.float32)


def prepare(table, packs):
    rows, width = table.shape
    block = min(rows, 2048)
    part = (packs[0].shape[0] - TAIL) // 3
    hidden = part * len(packs)
    whole = lambda shape: pl.BlockSpec(shape, lambda i: (0, 0))
    shapes = ((2 * width, hidden), (width, hidden), (hidden, width), (SUBLANES, hidden))
    types = (jnp.bfloat16, jnp.bfloat16, jnp.bfloat16, jnp.float32)
    return pl.pallas_call(
        functools.partial(prepare_kernel, part),
        grid=(rows // block,),
        in_specs=[pl.BlockSpec((block, width), lambda i: (i, 0))]
        + [whole(packs[0].shape)] * len(packs),
        out_specs=(pl.BlockSpec((block, width), lambda i: (i, 0)), *[whole(x) for x in shapes]),
        out_shape=(
            jax.ShapeDtypeStruct((rows, width), jnp.float32),
            *[jax.ShapeDtypeStruct(x, t) for x, t in zip(shapes, types)],
        ),
        compiler_params=pltpu.CompilerParams(vmem_limit_bytes=12 * 2**20),
        cost_estimate=pl.CostEstimate(flops=0, bytes_accessed=6 * rows * width, transcendentals=0),
    )(table, *packs)


def score_kernel(shard_rows, digits, tile_queries, follows, *refs):
    asked_ref, table_ref, mix_ref, first_ref, column_ref, bias_ref = refs[:6]
    (
        out_ref,
        sum_ref,
        query_ref,
        start_ref,
        key_ref,
        need_ref,
        flat_ref,
        total_ref,
        found_ref,
        place_ref,
        done,
    ) = refs[6 + follows :]
    width, rows = out_ref.shape
    feat = table_ref.shape[1]
    hidden_width = mix_ref.shape[1]
    tile = tile_queries * KIDS
    tiles = rows // tile_queries
    limit = width // 2 // SLOT

    ids = asked_ref[rows : 2 * rows, :].astype(jnp.int32)
    for d in range(2, digits + 1):
        ids = (ids << SHIFT) + asked_ref[d * rows : (d + 1) * rows, :].astype(jnp.int32)
    local = ids - lax.axis_index("blk") * shard_rows
    owned = (local >= 0) & (local < shard_rows)
    even = owned & ((local & 1) == 0)
    lane = lax.broadcasted_iota(jnp.int32, (rows, width), 1)
    earlier = (
        lax.broadcasted_iota(jnp.int32, (width, width), 0)
        < lax.broadcasted_iota(jnp.int32, (width, width), 1)
    ).astype(jnp.bfloat16)
    even_count = even.astype(jnp.float32)
    rank = jnp.dot(even_count.astype(jnp.bfloat16), earlier, preferred_element_type=jnp.float32)
    shift = lane - rank.astype(jnp.int32)
    word = jnp.where(even, (local >> 1) + (shift << FIELD) + (1 << (FIELD + 8)), 0)
    hop = 1
    while hop < width:
        bit = hop << FIELD
        moved = pltpu.roll(word, width - hop, 1)
        word = jnp.where((moved & bit) != 0, moved, jnp.where((word & bit) != 0, 0, word))
        hop *= 2
    front = word & ((1 << FIELD) - 1)
    slots = (front * 2).T
    for c in range(limit):
        flat_ref[c, :, 0:rows] = slots[c * SLOT : (c + 1) * SLOT, :]
    ahead = pltpu.make_async_copy(
        flat_ref.at[pl.ds(0, READY)], place_ref.at[pl.ds(0, READY)], done.at[0]
    )
    ahead.start()
    most = jnp.max(jnp.sum(even_count, axis=1, keepdims=True)).astype(jnp.int32)
    passes = (most + (SLOT - 1)) // SLOT
    need_ref[...] = jnp.where(word != 0, front, -1)
    key_ref[...] = jnp.where(owned, local, -4)
    queries = asked_ref[0:rows, :]
    query_ref[...] = queries.astype(jnp.float32)
    start_ref[...] = (
        jnp.dot(queries, first_ref[...], preferred_element_type=jnp.float32) + bias_ref[0:1, :]
    )
    sum_ref[...] = (
        lax.broadcasted_iota(jnp.int32, (tile_queries, tile), 1) // KIDS
        == lax.broadcasted_iota(jnp.int32, (tile_queries, tile), 0)
    ).astype(jnp.bfloat16)
    total_ref[...] = jnp.zeros(total_ref.shape, jnp.float32)
    ahead.wait()

    def gather(block, k):
        for i in range(tile_queries):
            for t in range(SLOT):
                at = pl.multiple_of(place_ref[block, t, k * tile_queries + i], 2)
                found_ref[k, pl.ds(i * KIDS + 2 * t, 2), :] = table_ref[pl.ds(at, 2), :]

    def score(c, k):
        some = slice(k * tile_queries, (k + 1) * tile_queries)
        nodes = found_ref[k]
        spread = jnp.broadcast_to(query_ref[some, :][:, None, :], (tile_queries, KIDS, feat))
        crossed = (nodes * spread.reshape(tile, feat)).astype(jnp.bfloat16)
        joined = jnp.concatenate([nodes.astype(jnp.bfloat16), crossed], axis=1)
        pre = jnp.dot(joined, mix_ref[...], preferred_element_type=jnp.float32)
        pre = pre.reshape(tile_queries, KIDS, hidden_width) + start_ref[some, :][:, None, :]
        hidden = jnp.maximum(pre.reshape(tile, hidden_width).astype(jnp.bfloat16), 0)
        score = jnp.dot(hidden, column_ref[...], preferred_element_type=jnp.float32)
        need = need_ref[some, :]
        if isinstance(c, int):
            need = need[:, c * SLOT : (c + 1) * SLOT]
        else:
            need = pltpu.roll(need, (width - c * SLOT) % width, 1)
        key = key_ref[some, :]
        above = key >> 1
        parity = key & 1
        code = jnp.full((tile_queries, width), -1, jnp.int32)
        for t in range(SLOT):
            code = jnp.where(above == need[:, t : t + 1], 2 * t + parity, code)
        slot = lax.broadcasted_iota(jnp.int32, (tile_queries, KIDS, width), 1)
        hit = code[:, None, :] == slot
        hits = jnp.where(hit, score.reshape(tile_queries, KIDS, width), 0.0)
        total_ref[some, :] += jnp.dot(
            sum_ref[...],
            hits.reshape(tile, width).astype(jnp.bfloat16),
            preferred_element_type=jnp.float32,
        )

    def one_pass(c, block):
        gather(block, 0)
        for k in range(tiles):
            if k + 1 < tiles:
                gather(block, k + 1)
            score(c, k)

    for c in range(READY):
        pl.when(passes > c)(functools.partial(one_pass, c, c))

    def later(c, carry):
        copy = pltpu.make_async_copy(flat_ref.at[c], place_ref.at[READY], done.at[1])
        copy.start()
        copy.wait()
        one_pass(c, READY)
        return carry

    lax.fori_loop(READY, passes, later, 0)
    out_ref[...] = total_ref[...].T.astype(out_ref.dtype)


def score_source(asked, rows, shard_rows, prepared, before):
    wide, mix, first, column, bias = prepared
    feat = asked.shape[1]
    hidden, width = column.shape
    digits = asked.shape[0] // rows - 1
    tile_queries = next(n for n in (32, 24, 16, 8) if rows % n == 0)
    tile = tile_queries * KIDS
    lanes = -(-rows // LANES) * LANES
    return pl.pallas_call(
        functools.partial(score_kernel, shard_rows, digits, tile_queries, len(before)),
        in_specs=[VMEM] * 6 + [pl.BlockSpec(memory_space=pl.ANY)] * len(before),
        out_specs=VMEM,
        out_shape=jax.ShapeDtypeStruct((width, rows), jnp.bfloat16),
        scratch_shapes=[
            pltpu.VMEM((tile_queries, tile), jnp.bfloat16),
            pltpu.VMEM((rows, feat), jnp.float32),
            pltpu.VMEM((rows, hidden), jnp.float32),
            pltpu.VMEM((rows, width), jnp.int32),
            pltpu.VMEM((rows, width), jnp.int32),
            pltpu.VMEM((width // 2 // SLOT, SLOT, lanes), jnp.int32),
            pltpu.VMEM((rows, width), jnp.float32),
            pltpu.VMEM((rows // tile_queries, tile, feat), jnp.float32),
            pltpu.SMEM((READY + 1, SLOT, lanes), jnp.int32),
            pltpu.SemaphoreType.DMA((2,)),
        ],
        compiler_params=pltpu.CompilerParams(vmem_limit_bytes=16 * 2**20),
        cost_estimate=pl.CostEstimate(
            flops=2 * rows * KIDS * 3 * feat * hidden,
            bytes_accessed=4 * rows * KIDS * feat,
            transcendentals=0,
        ),
    )(asked, wide, mix, first, column, bias, *before)


def mirrored(value, count):
    result = 0
    while count > 1:
        result = result * 2 + value % 2
        value //= 2
        count //= 2
    return result


def shards(queries, node_table, beam, w_query, w_node, w_cross, bias_hidden, w_out):
    groups = lax.axis_size("blk")
    parts = lax.axis_size("hid")
    rows, width = beam.shape
    feat = queries.shape[1]
    shard_rows = node_table.shape[0]
    binary = groups & (groups - 1) == 0 and parts & (parts - 1) == 0
    turns = groups // parts

    def far(value, back=False):
        pairs = []
        for b in range(groups):
            for h in range(parts):
                k = (mirrored(h, parts) if binary else h) * turns
                to = b ^ k if binary else (b + k if back else b - k) % groups
                pairs.append((b * parts + h, to * parts + h))
        return lax.ppermute(value, ("blk", "hid"), pairs)

    def near(value, turn, back=False):
        pairs = [
            (b, b ^ turn if binary else (b + turn if back else b - turn) % groups)
            for b in range(groups)
        ]
        return lax.ppermute(value, "blk", pairs)

    def across(value, step):
        pairs = [(h, h ^ step if binary else (h + step) % parts) for h in range(parts)]
        return lax.ppermute(value, "hid", pairs)

    digits = -(-(groups * shard_rows - 1).bit_length() // SHIFT)
    split = [
        ((beam >> (SHIFT * d)) & (2**SHIFT - 1)).astype(queries.dtype)
        for d in reversed(range(digits))
    ]
    first = far(jnp.concatenate([queries] + split, axis=0))

    part = w_out.shape[0]
    ends = jnp.stack([w_out, bias_hidden])
    ends = jnp.pad(ends, ((0, TAIL - 2), (0, feat - part)))
    weights = jnp.concatenate([w_query.T, w_node.T, w_cross.T, ends], axis=0)
    packs = [weights] + [across(weights, step) for step in range(1, parts)]
    prepared = prepare(node_table, packs)

    total, before = None, ()
    for turn in reversed(range(turns)):
        asked = near(first, turn) if turn else first
        scored = score_source(asked, rows, shard_rows, prepared, before)
        before = (scored,)
        back = (near(scored, turn, True) if turn else scored).astype(jnp.float32)
        total = back if total is None else total + back
    total = far(total.astype(jnp.bfloat16), True)

    own = lax.axis_index("hid")
    piece = width // parts
    result = lax.dynamic_slice_in_dim(total, own * piece, piece, axis=0).astype(jnp.float32)
    for step in range(1, parts):
        peer = own ^ step if binary else (own + step) % parts
        sent = lax.dynamic_slice_in_dim(total, peer * piece, piece, axis=0)
        result = result + across(sent, step).astype(jnp.float32)
    return result.T


def solution(mesh):
    in_specs = (
        P("blk", None),
        P("blk", None),
        P("blk", None),
        P(None, "hid"),
        P(None, "hid"),
        P(None, "hid"),
        P("hid"),
        P("hid"),
    )
    out_specs = P("blk", "hid")
    return jax.shard_map(shards, mesh=mesh, in_specs=in_specs, out_specs=out_specs, check_vma=False)
```

```python
import functools

import jax
import jax.numpy as jnp
from jax import lax
from jax.experimental import pallas as pl
from jax.experimental.pallas import tpu as pltpu
from jax.sharding import PartitionSpec as P


SLOT = 8
KIDS = 2 * SLOT
READY = 2
FIELD = 20
SHIFT = 8
LANES = 128
SUBLANES = 8
TAIL = 16

VMEM = pl.BlockSpec(memory_space=pltpu.VMEM)


def compose_kernel(digits, query_ref, beam_ref, message_ref):
    feat = query_ref.shape[1]
    width = beam_ref.shape[1]
    message_ref[:, 0:feat] = query_ref[...]
    ids = beam_ref[...]
    for d in range(digits):
        digit = (ids >> (SHIFT * (digits - 1 - d))) & (2**SHIFT - 1)
        begin = feat + d * width
        message_ref[:, begin : begin + width] = digit.astype(jnp.float32).astype(jnp.bfloat16)


def compose(queries, beam, digits):
    rows, feat = queries.shape
    width = beam.shape[1]
    return pl.pallas_call(
        functools.partial(compose_kernel, digits),
        in_specs=[VMEM, VMEM],
        out_specs=VMEM,
        out_shape=jax.ShapeDtypeStruct((rows, feat + digits * width), queries.dtype),
        compiler_params=pltpu.CompilerParams(vmem_limit_bytes=60 * 2**20),
    )(queries, beam)


def widen_kernel(table_ref, wide_ref):
    wide_ref[...] = table_ref[...].astype(jnp.float32)


def widen(table):
    rows, width = table.shape
    block = min(rows, 2048)
    spec = pl.BlockSpec((block, width), lambda i: (i, 0))
    return pl.pallas_call(
        widen_kernel,
        grid=(rows // block,),
        in_specs=[spec],
        out_specs=spec,
        out_shape=jax.ShapeDtypeStruct((rows, width), jnp.float32),
        compiler_params=pltpu.CompilerParams(vmem_limit_bytes=12 * 2**20),
        cost_estimate=pl.CostEstimate(flops=0, bytes_accessed=6 * rows * width, transcendentals=0),
    )(table)


def assemble_kernel(part, *refs):
    packs = refs[:-4]
    mix_ref, first_ref, column_ref, bias_ref = refs[-4:]
    feat = first_ref.shape[0]
    stacked = [
        jnp.concatenate([p[i * part : (i + 1) * part, :] for p in packs], axis=0) for i in range(3)
    ]
    first_ref[...] = stacked[0].T
    mix_ref[0:feat, :] = stacked[1].T
    mix_ref[feat:, :] = stacked[2].T
    ends = [p[3 * part :, :].astype(jnp.float32) for p in packs]
    out_row = jnp.concatenate([e[0:1, 0:part] for e in ends], axis=1)
    bias = jnp.concatenate([e[0:1, part : 2 * part] for e in ends], axis=1)
    column_ref[...] = jnp.broadcast_to(out_row, (feat, out_row.shape[1])).T.astype(jnp.bfloat16)
    bias_ref[...] = jnp.broadcast_to(bias, bias_ref.shape)


def assemble(packs):
    width = packs[0].shape[1]
    part = (packs[0].shape[0] - TAIL) // 3
    hidden = part * len(packs)
    return pl.pallas_call(
        functools.partial(assemble_kernel, part),
        in_specs=[VMEM] * len(packs),
        out_specs=(VMEM,) * 4,
        out_shape=(
            jax.ShapeDtypeStruct((2 * width, hidden), jnp.bfloat16),
            jax.ShapeDtypeStruct((width, hidden), jnp.bfloat16),
            jax.ShapeDtypeStruct((hidden, width), jnp.bfloat16),
            jax.ShapeDtypeStruct((SUBLANES, hidden), jnp.float32),
        ),
        compiler_params=pltpu.CompilerParams(vmem_limit_bytes=4 * 2**20),
        cost_estimate=pl.CostEstimate(
            flops=0, bytes_accessed=8 * width * hidden, transcendentals=0
        ),
    )(*packs)


def score_kernel(shard_rows, digits, tile_queries, follows, *refs):
    asked_ref, table_ref, mix_ref, first_ref, column_ref, bias_ref = refs[:6]
    (
        out_ref,
        sum_ref,
        query_ref,
        start_ref,
        key_ref,
        need_ref,
        flat_ref,
        total_ref,
        found_ref,
        place_ref,
        done,
    ) = refs[6 + follows :]
    width, rows = out_ref.shape
    feat = table_ref.shape[1]
    hidden_width = mix_ref.shape[1]
    tile = tile_queries * KIDS
    tiles = rows // tile_queries
    limit = width // 2 // SLOT

    ids = asked_ref[:, feat : feat + width].astype(jnp.int32)
    for d in range(1, digits):
        begin = feat + d * width
        ids = (ids << SHIFT) + asked_ref[:, begin : begin + width].astype(jnp.int32)
    local = ids - lax.axis_index("blk") * shard_rows
    owned = (local >= 0) & (local < shard_rows)
    even = owned & ((local & 1) == 0)
    lane = lax.broadcasted_iota(jnp.int32, (rows, width), 1)
    earlier = (
        lax.broadcasted_iota(jnp.int32, (width, width), 0)
        < lax.broadcasted_iota(jnp.int32, (width, width), 1)
    ).astype(jnp.bfloat16)
    even_count = even.astype(jnp.float32)
    rank = jnp.dot(even_count.astype(jnp.bfloat16), earlier, preferred_element_type=jnp.float32)
    shift = lane - rank.astype(jnp.int32)
    word = jnp.where(even, (local >> 1) + (shift << FIELD) + (1 << (FIELD + 8)), 0)
    hop = 1
    while hop < width:
        bit = hop << FIELD
        moved = pltpu.roll(word, width - hop, 1)
        word = jnp.where((moved & bit) != 0, moved, jnp.where((word & bit) != 0, 0, word))
        hop *= 2
    front = word & ((1 << FIELD) - 1)
    slots = (front * 2).T
    for c in range(limit):
        flat_ref[c, :, 0:rows] = slots[c * SLOT : (c + 1) * SLOT, :]
    ahead = pltpu.make_async_copy(
        flat_ref.at[pl.ds(0, READY)], place_ref.at[pl.ds(0, READY)], done.at[0]
    )
    ahead.start()
    most = jnp.max(jnp.sum(even_count, axis=1, keepdims=True)).astype(jnp.int32)
    passes = (most + (SLOT - 1)) // SLOT
    need_ref[...] = jnp.where(word != 0, front, -1)
    key_ref[...] = jnp.where(owned, local, -4)
    queries = asked_ref[:, 0:feat]
    query_ref[...] = queries.astype(jnp.float32)
    start_ref[...] = (
        jnp.dot(queries, first_ref[...], preferred_element_type=jnp.float32) + bias_ref[0:1, :]
    )
    sum_ref[...] = (
        lax.broadcasted_iota(jnp.int32, (tile_queries, tile), 1) // KIDS
        == lax.broadcasted_iota(jnp.int32, (tile_queries, tile), 0)
    ).astype(jnp.bfloat16)
    total_ref[...] = jnp.zeros(total_ref.shape, jnp.float32)
    ahead.wait()

    def gather(block, k):
        for i in range(tile_queries):
            for t in range(SLOT):
                at = pl.multiple_of(place_ref[block, t, k * tile_queries + i], 2)
                found_ref[k, pl.ds(i * KIDS + 2 * t, 2), :] = table_ref[pl.ds(at, 2), :]

    def score(c, k):
        some = slice(k * tile_queries, (k + 1) * tile_queries)
        nodes = found_ref[k]
        spread = jnp.broadcast_to(query_ref[some, :][:, None, :], (tile_queries, KIDS, feat))
        crossed = (nodes * spread.reshape(tile, feat)).astype(jnp.bfloat16)
        joined = jnp.concatenate([nodes.astype(jnp.bfloat16), crossed], axis=1)
        pre = jnp.dot(joined, mix_ref[...], preferred_element_type=jnp.float32)
        pre = pre.reshape(tile_queries, KIDS, hidden_width) + start_ref[some, :][:, None, :]
        hidden = jnp.maximum(pre.reshape(tile, hidden_width).astype(jnp.bfloat16), 0)
        score = jnp.dot(hidden, column_ref[...], preferred_element_type=jnp.float32)
        need = need_ref[some, :]
        if isinstance(c, int):
            need = need[:, c * SLOT : (c + 1) * SLOT]
        else:
            need = pltpu.roll(need, (width - c * SLOT) % width, 1)
        key = key_ref[some, :]
        above = key >> 1
        parity = key & 1
        code = jnp.full((tile_queries, width), -1, jnp.int32)
        for t in range(SLOT):
            code = jnp.where(above == need[:, t : t + 1], 2 * t + parity, code)
        slot = lax.broadcasted_iota(jnp.int32, (tile_queries, KIDS, width), 1)
        hit = code[:, None, :] == slot
        hits = jnp.where(hit, score.reshape(tile_queries, KIDS, width), 0.0)
        total_ref[some, :] += jnp.dot(
            sum_ref[...],
            hits.reshape(tile, width).astype(jnp.bfloat16),
            preferred_element_type=jnp.float32,
        )

    def one_pass(c, block):
        gather(block, 0)
        for k in range(tiles):
            if k + 1 < tiles:
                gather(block, k + 1)
            score(c, k)

    for c in range(READY):
        pl.when(passes > c)(functools.partial(one_pass, c, c))

    def later(c, carry):
        copy = pltpu.make_async_copy(flat_ref.at[c], place_ref.at[READY], done.at[1])
        copy.start()
        copy.wait()
        one_pass(c, READY)
        return carry

    lax.fori_loop(READY, passes, later, 0)
    out_ref[...] = total_ref[...].T.astype(out_ref.dtype)


def score_source(asked, rows, shard_rows, prepared, before):
    wide, mix, first, column, bias = prepared
    feat = wide.shape[1]
    hidden, width = column.shape
    digits = (asked.shape[1] - feat) // width
    tile_queries = next(n for n in (32, 24, 16, 8) if rows % n == 0)
    tile = tile_queries * KIDS
    lanes = -(-rows // LANES) * LANES
    return pl.pallas_call(
        functools.partial(score_kernel, shard_rows, digits, tile_queries, len(before)),
        in_specs=[VMEM] * 6 + [pl.BlockSpec(memory_space=pl.ANY)] * len(before),
        out_specs=VMEM,
        out_shape=jax.ShapeDtypeStruct((width, rows), jnp.bfloat16),
        scratch_shapes=[
            pltpu.VMEM((tile_queries, tile), jnp.bfloat16),
            pltpu.VMEM((rows, feat), jnp.float32),
            pltpu.VMEM((rows, hidden), jnp.float32),
            pltpu.VMEM((rows, width), jnp.int32),
            pltpu.VMEM((rows, width), jnp.int32),
            pltpu.VMEM((width // 2 // SLOT, SLOT, lanes), jnp.int32),
            pltpu.VMEM((rows, width), jnp.float32),
            pltpu.VMEM((rows // tile_queries, tile, feat), jnp.float32),
            pltpu.SMEM((READY + 1, SLOT, lanes), jnp.int32),
            pltpu.SemaphoreType.DMA((2,)),
        ],
        compiler_params=pltpu.CompilerParams(vmem_limit_bytes=16 * 2**20),
        cost_estimate=pl.CostEstimate(
            flops=2 * rows * KIDS * 3 * feat * hidden,
            bytes_accessed=4 * rows * KIDS * feat,
            transcendentals=0,
        ),
    )(asked, wide, mix, first, column, bias, *before)


def mirrored(value, count):
    result = 0
    while count > 1:
        result = result * 2 + value % 2
        value //= 2
        count //= 2
    return result


def shards(queries, node_table, beam, w_query, w_node, w_cross, bias_hidden, w_out):
    groups = lax.axis_size("blk")
    parts = lax.axis_size("hid")
    rows, width = beam.shape
    feat = queries.shape[1]
    shard_rows = node_table.shape[0]
    binary = groups & (groups - 1) == 0 and parts & (parts - 1) == 0
    turns = groups // parts

    def far(value, back=False):
        pairs = []
        for b in range(groups):
            for h in range(parts):
                k = (mirrored(h, parts) if binary else h) * turns
                to = b ^ k if binary else (b + k if back else b - k) % groups
                pairs.append((b * parts + h, to * parts + h))
        return lax.ppermute(value, ("blk", "hid"), pairs)

    def near(value, turn, back=False):
        pairs = [
            (b, b ^ turn if binary else (b + turn if back else b - turn) % groups)
            for b in range(groups)
        ]
        return lax.ppermute(value, "blk", pairs)

    def across(value, step):
        pairs = [(h, h ^ step if binary else (h + step) % parts) for h in range(parts)]
        return lax.ppermute(value, "hid", pairs)

    digits = -(-(groups * shard_rows - 1).bit_length() // SHIFT)
    first = far(compose(queries, beam, digits))

    part = w_out.shape[0]
    ends = jnp.concatenate([w_out, bias_hidden])[None]
    ends = jnp.pad(ends, ((0, TAIL - 1), (0, feat - 2 * part)))
    weights = jnp.concatenate([w_query.T, w_node.T, w_cross.T, ends], axis=0)
    packs = [weights] + [across(weights, step) for step in range(1, parts)]
    wide = widen(node_table)
    prepared = (wide, *assemble(packs))

    total, before = None, ()
    for turn in reversed(range(turns)):
        asked = near(first, turn) if turn else first
        scored = score_source(asked, rows, shard_rows, prepared, before)
        before = (scored,)
        back = (near(scored, turn, True) if turn else scored).astype(jnp.float32)
        total = back if total is None else total + back
    total = far(total.astype(jnp.bfloat16), True)

    own = lax.axis_index("hid")
    piece = width // parts
    result = lax.dynamic_slice_in_dim(total, own * piece, piece, axis=0).astype(jnp.float32)
    for step in range(1, parts):
        peer = own ^ step if binary else (own + step) % parts
        sent = lax.dynamic_slice_in_dim(total, peer * piece, piece, axis=0)
        result = result + across(sent, step).astype(jnp.float32)
    return result.T


def solution(mesh):
    in_specs = (
        P("blk", None),
        P("blk", None),
        P("blk", None),
        P(None, "hid"),
        P(None, "hid"),
        P(None, "hid"),
        P("hid"),
        P("hid"),
    )
    out_specs = P("blk", "hid")
    return jax.shard_map(shards, mesh=mesh, in_specs=in_specs, out_specs=out_specs, check_vma=False)
```

```python
import functools

import jax
import jax.numpy as jnp
from jax import lax
from jax.experimental import pallas as pl
from jax.experimental.pallas import tpu as pltpu
from jax.sharding import PartitionSpec as P


SLOT = 8
KIDS = 2 * SLOT
READY = 2
FIELD = 20
SHIFT = 8
LANES = 128
SUBLANES = 8
STATIC = 2

VMEM = pl.BlockSpec(memory_space=pltpu.VMEM)


def pack_kernel(digits, *refs):
    sources, (message_ref, pack_ref), held, done = refs[:7], refs[7:9], refs[9:-1], refs[-1]
    copies = [
        pltpu.make_async_copy(source, target, done.at[i])
        for i, (source, target) in enumerate(zip(sources, held))
    ]
    for copy in copies:
        copy.start()
    beam_ref, query_ref = held[:2]
    weights, (out_row, bias_row) = held[2:5], held[5:7]
    rows = beam_ref.shape[0]
    part = weights[0].shape[0]
    width = pack_ref.shape[1]
    for copy in copies:
        copy.wait()
    ids = beam_ref[...]
    for d in range(digits):
        digit = (ids >> (SHIFT * (digits - 1 - d))) & (2**SHIFT - 1)
        message_ref[(d + 1) * rows : (d + 2) * rows, :] = digit.astype(jnp.float32).astype(
            jnp.bfloat16
        )
    message_ref[0:rows, :] = query_ref[...]
    for i, weight in enumerate(weights):
        pack_ref[i * part : (i + 1) * part, :] = weight[...]
    tail = pack_ref.shape[0] - 3 * part
    ends = jnp.concatenate(
        [
            out_row[...].astype(jnp.float32),
            bias_row[...].astype(jnp.float32),
            jnp.zeros((tail - 2, part), jnp.float32),
        ],
        axis=0,
    )
    ends = jnp.concatenate([ends, jnp.zeros((tail, width - part), jnp.float32)], axis=1)
    pack_ref[3 * part :, :] = ends.astype(jnp.bfloat16)


def pack(queries, beam, digits, weights, w_out, bias):
    rows, width = queries.shape
    part = w_out.shape[0]
    given = (beam, queries, *[w.T for w in weights], w_out[None, :], bias[None, :])
    return pl.pallas_call(
        functools.partial(pack_kernel, digits),
        in_specs=[pl.BlockSpec(memory_space=pltpu.HBM)] * len(given),
        out_specs=(VMEM, VMEM),
        out_shape=(
            jax.ShapeDtypeStruct(((digits + 1) * rows, width), jnp.bfloat16),
            jax.ShapeDtypeStruct((3 * part + 16, width), jnp.bfloat16),
        ),
        scratch_shapes=[pltpu.VMEM(x.shape, x.dtype) for x in given]
        + [pltpu.SemaphoreType.DMA((len(given),))],
        compiler_params=pltpu.CompilerParams(vmem_limit_bytes=60 * 2**20),
    )(*given)


def widen_kernel(chunks, table_ref, wide_ref, held_ref, done):
    rows = table_ref.shape[0] // chunks
    copies = [
        pltpu.make_async_copy(
            table_ref.at[pl.ds(i * rows, rows)], held_ref.at[pl.ds(i * rows, rows)], done.at[i]
        )
        for i in range(chunks)
    ]
    for copy in copies:
        copy.start()
    for i, copy in enumerate(copies):
        copy.wait()
        some = slice(i * rows, (i + 1) * rows)
        wide_ref[some, :] = held_ref[some, :].astype(jnp.float32)


def widen(table):
    rows, width = table.shape
    chunks = 8
    return pl.pallas_call(
        functools.partial(widen_kernel, chunks),
        in_specs=[pl.BlockSpec(memory_space=pltpu.HBM)],
        out_specs=VMEM,
        out_shape=jax.ShapeDtypeStruct((rows, width), jnp.float32),
        scratch_shapes=[pltpu.VMEM((rows, width), table.dtype), pltpu.SemaphoreType.DMA((chunks,))],
        compiler_params=pltpu.CompilerParams(vmem_limit_bytes=12 * 2**20),
        cost_estimate=pl.CostEstimate(flops=0, bytes_accessed=6 * rows * width, transcendentals=0),
    )(table)


def score_kernel(shard_rows, digits, turns, parts, tile_queries, *refs):
    asked, table_ref, packs = refs[:turns], refs[turns], refs[turns + 1 : turns + 1 + parts]
    outs = refs[turns + 1 + parts : 2 * turns + 1 + parts]
    (
        mix_ref,
        out_row_ref,
        sum_ref,
        query_ref,
        start_ref,
        key_ref,
        need_ref,
        flat_ref,
        total_ref,
        found_ref,
        place_ref,
        passes_ref,
        done,
    ) = refs[2 * turns + 1 + parts :]
    width, rows = outs[0].shape
    feat = table_ref.shape[1]
    hidden_width = mix_ref.shape[1]
    part = hidden_width // parts
    tile = tile_queries * KIDS
    tiles = rows // tile_queries
    limit = width // 2 // SLOT

    ids = jnp.concatenate([a[rows : 2 * rows, :] for a in asked], axis=0).astype(jnp.int32)
    for d in range(2, digits + 1):
        digit = jnp.concatenate([a[d * rows : (d + 1) * rows, :] for a in asked], axis=0)
        ids = (ids << SHIFT) + digit.astype(jnp.int32)
    local = ids - lax.axis_index("blk") * shard_rows
    owned = (local >= 0) & (local < shard_rows)
    even = owned & ((local & 1) == 0)
    lane = lax.broadcasted_iota(jnp.int32, (turns * rows, width), 1)
    earlier = (
        lax.broadcasted_iota(jnp.int32, (width, width), 0)
        < lax.broadcasted_iota(jnp.int32, (width, width), 1)
    ).astype(jnp.bfloat16)
    even_count = even.astype(jnp.float32)
    rank = jnp.dot(even_count.astype(jnp.bfloat16), earlier, preferred_element_type=jnp.float32)
    shift = lane - rank.astype(jnp.int32)
    word = jnp.where(even, (local >> 1) + (shift << FIELD) + (1 << (FIELD + 8)), 0)
    hop = 1
    while hop < width:
        bit = hop << FIELD
        moved = pltpu.roll(word, width - hop, 1)
        word = jnp.where((moved & bit) != 0, moved, jnp.where((word & bit) != 0, 0, word))
        hop *= 2
    front = word & ((1 << FIELD) - 1)
    ahead = []
    for j in range(turns):
        slots = (front[j * rows : (j + 1) * rows, :] * 2).T
        for c in range(limit):
            flat_ref[j * limit + c, :, 0:rows] = slots[c * SLOT : (c + 1) * SLOT, :]
        ahead.append(
            pltpu.make_async_copy(
                flat_ref.at[pl.ds(j * limit, READY)],
                place_ref.at[pl.ds(j * READY, READY)],
                done.at[j],
            )
        )
        ahead[-1].start()
        most = jnp.max(
            jnp.sum(even_count[j * rows : (j + 1) * rows, :], axis=1, keepdims=True)
        ).astype(jnp.int32)
        passes_ref[j] = (most + (SLOT - 1)) // SLOT
    need_ref[...] = jnp.where(word != 0, front, -1)
    key_ref[...] = jnp.where(owned, local, -4)

    stacked = [
        jnp.concatenate([p[i * part : (i + 1) * part, :] for p in packs], axis=0) for i in range(3)
    ]
    mix_ref[0:feat, :] = stacked[1].T
    mix_ref[feat:, :] = stacked[2].T
    ends = [p[3 * part :, :].astype(jnp.float32) for p in packs]
    out_row = jnp.concatenate([e[0:1, 0:part] for e in ends], axis=1)
    bias = jnp.concatenate([e[1:2, 0:part] for e in ends], axis=1)
    out_row_ref[...] = jnp.broadcast_to(out_row, out_row_ref.shape)
    queries = jnp.concatenate([a[0:rows, :] for a in asked], axis=0)
    query_ref[...] = queries.astype(jnp.float32)
    start_ref[...] = (
        jnp.dot(queries, stacked[0].T, preferred_element_type=jnp.float32) + bias
    )
    sum_ref[...] = (
        lax.broadcasted_iota(jnp.int32, (tile_queries, tile), 1) // KIDS
        == lax.broadcasted_iota(jnp.int32, (tile_queries, tile), 0)
    ).astype(jnp.bfloat16)
    total_ref[...] = jnp.zeros(total_ref.shape, jnp.float32)
    for copy in ahead:
        copy.wait()

    def gather(block, k):
        for i in range(tile_queries):
            for t in range(SLOT):
                at = pl.multiple_of(place_ref[block, t, k * tile_queries + i], 2)
                found_ref[k, pl.ds(i * KIDS + 2 * t, 2), :] = table_ref[pl.ds(at, 2), :]

    def queries_of(j, k):
        if isinstance(j, int):
            return slice(j * rows + k * tile_queries, j * rows + (k + 1) * tile_queries)
        return pl.ds(pl.multiple_of(j * rows + k * tile_queries, SUBLANES), tile_queries)

    def score(j, k):
        some = queries_of(j, k)
        nodes = found_ref[k]
        spread = jnp.broadcast_to(query_ref[some, :][:, None, :], (tile_queries, KIDS, feat))
        crossed = (nodes * spread.reshape(tile, feat)).astype(jnp.bfloat16)
        joined = jnp.concatenate([nodes.astype(jnp.bfloat16), crossed], axis=1)
        pre = jnp.dot(joined, mix_ref[...], preferred_element_type=jnp.float32)
        pre = pre.reshape(tile_queries, KIDS, hidden_width) + start_ref[some, :][:, None, :]
        weighed = jnp.maximum(pre.reshape(tile, hidden_width), 0.0) * out_row_ref[0:1, :]
        return jnp.sum(weighed, axis=1, keepdims=True)

    def settle(j, c, k, scores):
        some = queries_of(j, k)
        need = need_ref[some, :]
        if isinstance(c, int):
            need = need[:, c * SLOT : (c + 1) * SLOT]
        else:
            need = pltpu.roll(need, (width - c * SLOT) % width, 1)
        key = key_ref[some, :]
        above = key >> 1
        parity = key & 1
        code = jnp.full((tile_queries, width), -1, jnp.int32)
        for t in range(SLOT):
            code = jnp.where(above == need[:, t : t + 1], 2 * t + parity, code)
        slot = lax.broadcasted_iota(jnp.int32, (tile_queries, KIDS, width), 1)
        hits = jnp.where(code[:, None, :] == slot, scores.reshape(tile_queries, KIDS, 1), 0.0)
        total_ref[some, :] += jnp.dot(
            sum_ref[...],
            hits.reshape(tile, width).astype(jnp.bfloat16),
            preferred_element_type=jnp.float32,
        )

    def one_pass(j, c, block):
        gather(block, 0)
        before = None
        for k in range(tiles):
            if k + 1 < tiles:
                gather(block, k + 1)
            scores = score(j, k)
            if k > 0:
                settle(j, c, k - 1, before)
            before = scores
        settle(j, c, tiles - 1, before)

    def late_pass(j, c):
        copy = pltpu.make_async_copy(
            flat_ref.at[j * limit + c], place_ref.at[turns * READY], done.at[turns]
        )
        copy.start()
        copy.wait()
        one_pass(j, c, turns * READY)

    if turns <= STATIC:
        for j in range(turns):
            for c in range(READY):
                pl.when(passes_ref[j] > c)(functools.partial(one_pass, j, c, j * READY + c))

            def later(c, carry, j=j):
                late_pass(j, c)
                return carry

            lax.fori_loop(READY, passes_ref[j], later, 0)
    else:

        def one_source(j, carry):
            def every(c, inner):
                late_pass(j, c)
                return inner

            return lax.fori_loop(0, passes_ref[j], every, carry)

        lax.fori_loop(0, turns, one_source, 0)
    for j, out_ref in enumerate(outs):
        out_ref[...] = total_ref[j * rows : (j + 1) * rows, :].T.astype(out_ref.dtype)


def score_sources(asked, rows, shard_rows, wide, packs):
    turns = len(asked)
    feat = asked[0].shape[1]
    width = feat
    digits = asked[0].shape[0] // rows - 1
    part = (packs[0].shape[0] - 16) // 3
    hidden = part * len(packs)
    tile_queries = next(n for n in (48, 32, 24, 16, 8) if rows % n == 0)
    tile = tile_queries * KIDS
    lanes = -(-rows // LANES) * LANES
    count = turns * rows
    return pl.pallas_call(
        functools.partial(score_kernel, shard_rows, digits, turns, len(packs), tile_queries),
        in_specs=[VMEM] * (turns + 1 + len(packs)),
        out_specs=(VMEM,) * turns,
        out_shape=(jax.ShapeDtypeStruct((width, rows), jnp.bfloat16),) * turns,
        scratch_shapes=[
            pltpu.VMEM((2 * feat, hidden), jnp.bfloat16),
            pltpu.VMEM((SUBLANES, hidden), jnp.float32),
            pltpu.VMEM((tile_queries, tile), jnp.bfloat16),
            pltpu.VMEM((count, feat), jnp.float32),
            pltpu.VMEM((count, hidden), jnp.float32),
            pltpu.VMEM((count, width), jnp.int32),
            pltpu.VMEM((count, width), jnp.int32),
            pltpu.VMEM((turns * (width // 2 // SLOT), SLOT, lanes), jnp.int32),
            pltpu.VMEM((count, width), jnp.float32),
            pltpu.VMEM((rows // tile_queries, tile, feat), jnp.float32),
            pltpu.SMEM((turns * READY + 1, SLOT, lanes), jnp.int32),
            pltpu.SMEM((turns,), jnp.int32),
            pltpu.SemaphoreType.DMA((turns + 1,)),
        ],
        compiler_params=pltpu.CompilerParams(vmem_limit_bytes=16 * 2**20),
        cost_estimate=pl.CostEstimate(
            flops=2 * count * KIDS * 3 * feat * hidden,
            bytes_accessed=4 * count * KIDS * feat,
            transcendentals=0,
        ),
    )(*asked, wide, *packs)


def mirrored(value, count):
    result = 0
    while count > 1:
        result = result * 2 + value % 2
        value //= 2
        count //= 2
    return result


def far_first(count):
    return sorted(range(1, count), key=lambda step: (step < 2, step))


def shards(queries, node_table, beam, w_query, w_node, w_cross, bias_hidden, w_out):
    groups = lax.axis_size("blk")
    parts = lax.axis_size("hid")
    rows, width = beam.shape
    shard_rows = node_table.shape[0]
    binary = groups & (groups - 1) == 0 and parts & (parts - 1) == 0
    turns = groups // parts

    def hop_pairs(turn, back):
        pairs = []
        for b in range(groups):
            for h in range(parts):
                k = (mirrored(h, parts) if binary else h) * turns + turn
                if binary:
                    to = b ^ k
                else:
                    to = (b - k) % groups if not back else (b + k) % groups
                pairs.append((b * parts + h, to * parts + h))
        return pairs

    def hop(value, turn, back=False):
        return lax.ppermute(value, ("blk", "hid"), hop_pairs(turn, back))

    def across(value, step):
        pairs = [(h, h ^ step if binary else (h + step) % parts) for h in range(parts)]
        return lax.ppermute(value, "hid", pairs)

    digits = -(-(groups * shard_rows - 1).bit_length() // SHIFT)
    message, weights = pack(queries, beam, digits, (w_query, w_node, w_cross), w_out, bias_hidden)
    asked = [hop(message, turn) for turn in range(turns)]
    packs = [weights] + [across(weights, step) for step in far_first(parts)]
    scored = score_sources(asked, rows, shard_rows, widen(node_table), packs)
    total = sum(hop(s, turn, True).astype(jnp.float32) for turn, s in enumerate(scored))

    own = lax.axis_index("hid")
    piece = width // parts
    result = lax.dynamic_slice_in_dim(total, own * piece, piece, axis=0)
    for step in far_first(parts):
        peer = own ^ step if binary else (own + step) % parts
        sent = lax.dynamic_slice_in_dim(total, peer * piece, piece, axis=0)
        result = result + across(sent.astype(jnp.bfloat16), step).astype(jnp.float32)
    return result.T


def solution(mesh):
    in_specs = (
        P("blk", None),
        P("blk", None),
        P("blk", None),
        P(None, "hid"),
        P(None, "hid"),
        P(None, "hid"),
        P("hid"),
        P("hid"),
    )
    out_specs = P("blk", "hid")
    return jax.shard_map(shards, mesh=mesh, in_specs=in_specs, out_specs=out_specs, check_vma=False)
```

```python
import functools

import jax
import jax.numpy as jnp
from jax import lax
from jax.experimental import pallas as pl
from jax.experimental.pallas import tpu as pltpu
from jax.sharding import PartitionSpec as P


SLOT = 8
KIDS = 2 * SLOT
READY = 2
FIELD = 20
SHIFT = 8
LANES = 128
SUBLANES = 8
STATIC = 2

VMEM = pl.BlockSpec(memory_space=pltpu.VMEM)


def pack_kernel(digits, *refs):
    sources, (message_ref, pack_ref), held, done = refs[:7], refs[7:9], refs[9:-1], refs[-1]
    copies = [
        pltpu.make_async_copy(source, target, done.at[i])
        for i, (source, target) in enumerate(zip(sources, held))
    ]
    for copy in copies:
        copy.start()
    beam_ref, query_ref = held[:2]
    weights, (out_row, bias_row) = held[2:5], held[5:7]
    rows = beam_ref.shape[0]
    part = weights[0].shape[0]
    width = pack_ref.shape[1]
    for copy in copies:
        copy.wait()
    ids = beam_ref[...]
    for d in range(digits):
        digit = (ids >> (SHIFT * (digits - 1 - d))) & (2**SHIFT - 1)
        message_ref[(d + 1) * rows : (d + 2) * rows, :] = digit.astype(jnp.float32).astype(
            jnp.bfloat16
        )
    message_ref[0:rows, :] = query_ref[...]
    for i, weight in enumerate(weights):
        pack_ref[i * part : (i + 1) * part, :] = weight[...]
    tail = pack_ref.shape[0] - 3 * part
    ends = jnp.concatenate(
        [
            out_row[...].astype(jnp.float32),
            bias_row[...].astype(jnp.float32),
            jnp.zeros((tail - 2, part), jnp.float32),
        ],
        axis=0,
    )
    ends = jnp.concatenate([ends, jnp.zeros((tail, width - part), jnp.float32)], axis=1)
    pack_ref[3 * part :, :] = ends.astype(jnp.bfloat16)


def pack(queries, beam, digits, weights, w_out, bias):
    rows, width = queries.shape
    part = w_out.shape[0]
    given = (beam, queries, *[w.T for w in weights], w_out[None, :], bias[None, :])
    return pl.pallas_call(
        functools.partial(pack_kernel, digits),
        in_specs=[pl.BlockSpec(memory_space=pltpu.HBM)] * len(given),
        out_specs=(VMEM, VMEM),
        out_shape=(
            jax.ShapeDtypeStruct(((digits + 1) * rows, width), jnp.bfloat16),
            jax.ShapeDtypeStruct((3 * part + 16, width), jnp.bfloat16),
        ),
        scratch_shapes=[pltpu.VMEM(x.shape, x.dtype) for x in given]
        + [pltpu.SemaphoreType.DMA((len(given),))],
        compiler_params=pltpu.CompilerParams(vmem_limit_bytes=60 * 2**20),
    )(*given)


def widen_kernel(chunks, table_ref, wide_ref, held_ref, done):
    rows = table_ref.shape[0] // chunks
    copies = [
        pltpu.make_async_copy(
            table_ref.at[pl.ds(i * rows, rows)], held_ref.at[pl.ds(i * rows, rows)], done.at[i]
        )
        for i in range(chunks)
    ]
    for copy in copies:
        copy.start()
    for i, copy in enumerate(copies):
        copy.wait()
        some = slice(i * rows, (i + 1) * rows)
        wide_ref[some, :] = held_ref[some, :].astype(jnp.float32)


def widen(table):
    rows, width = table.shape
    chunks = 8
    return pl.pallas_call(
        functools.partial(widen_kernel, chunks),
        in_specs=[pl.BlockSpec(memory_space=pltpu.HBM)],
        out_specs=VMEM,
        out_shape=jax.ShapeDtypeStruct((rows, width), jnp.float32),
        scratch_shapes=[pltpu.VMEM((rows, width), table.dtype), pltpu.SemaphoreType.DMA((chunks,))],
        compiler_params=pltpu.CompilerParams(vmem_limit_bytes=12 * 2**20),
        cost_estimate=pl.CostEstimate(flops=0, bytes_accessed=6 * rows * width, transcendentals=0),
    )(table)


def score_kernel(shard_rows, digits, turns, parts, tile_queries, *refs):
    asked, table_ref, packs = refs[:turns], refs[turns], refs[turns + 1 : turns + 1 + parts]
    outs = refs[turns + 1 + parts : 2 * turns + 1 + parts]
    (
        mix_ref,
        out_row_ref,
        sum_ref,
        query_ref,
        start_ref,
        key_ref,
        need_ref,
        flat_ref,
        total_ref,
        found_ref,
        place_ref,
        passes_ref,
        done,
    ) = refs[2 * turns + 1 + parts :]
    width, rows = outs[0].shape
    feat = table_ref.shape[1]
    hidden_width = mix_ref.shape[1]
    part = hidden_width // parts
    tile = tile_queries * KIDS
    tiles = rows // tile_queries
    limit = width // 2 // SLOT

    ids = jnp.concatenate([a[rows : 2 * rows, :] for a in asked], axis=0).astype(jnp.int32)
    for d in range(2, digits + 1):
        digit = jnp.concatenate([a[d * rows : (d + 1) * rows, :] for a in asked], axis=0)
        ids = (ids << SHIFT) + digit.astype(jnp.int32)
    local = ids - lax.axis_index("blk") * shard_rows
    owned = (local >= 0) & (local < shard_rows)
    even = owned & ((local & 1) == 0)
    lane = lax.broadcasted_iota(jnp.int32, (turns * rows, width), 1)
    earlier = (
        lax.broadcasted_iota(jnp.int32, (width, width), 0)
        < lax.broadcasted_iota(jnp.int32, (width, width), 1)
    ).astype(jnp.bfloat16)
    even_count = even.astype(jnp.float32)
    rank = jnp.dot(even_count.astype(jnp.bfloat16), earlier, preferred_element_type=jnp.float32)
    shift = lane - rank.astype(jnp.int32)
    word = jnp.where(even, (local >> 1) + (shift << FIELD) + (1 << (FIELD + 8)), 0)
    hop = 1
    while hop < width:
        bit = hop << FIELD
        moved = pltpu.roll(word, width - hop, 1)
        word = jnp.where((moved & bit) != 0, moved, jnp.where((word & bit) != 0, 0, word))
        hop *= 2
    front = word & ((1 << FIELD) - 1)
    ahead = []
    for j in range(turns):
        slots = (front[j * rows : (j + 1) * rows, :] * 2).T
        for c in range(limit):
            flat_ref[j * limit + c, :, 0:rows] = slots[c * SLOT : (c + 1) * SLOT, :]
        ahead.append(
            pltpu.make_async_copy(
                flat_ref.at[pl.ds(j * limit, READY)],
                place_ref.at[pl.ds(j * READY, READY)],
                done.at[j],
            )
        )
        ahead[-1].start()
        most = jnp.max(
            jnp.sum(even_count[j * rows : (j + 1) * rows, :], axis=1, keepdims=True)
        ).astype(jnp.int32)
        passes_ref[j] = (most + (SLOT - 1)) // SLOT
    need_ref[...] = jnp.where(word != 0, front, -1)
    key_ref[...] = jnp.where(owned, local, -4)

    stacked = [
        jnp.concatenate([p[i * part : (i + 1) * part, :] for p in packs], axis=0) for i in range(3)
    ]
    mix_ref[0:feat, :] = stacked[1].T
    mix_ref[feat:, :] = stacked[2].T
    ends = [p[3 * part :, :].astype(jnp.float32) for p in packs]
    out_row = jnp.concatenate([e[0:1, 0:part] for e in ends], axis=1)
    bias = jnp.concatenate([e[1:2, 0:part] for e in ends], axis=1)
    out_row_ref[...] = jnp.broadcast_to(out_row, out_row_ref.shape)
    queries = jnp.concatenate([a[0:rows, :] for a in asked], axis=0)
    query_ref[...] = queries.astype(jnp.float32)
    start_ref[...] = (
        jnp.dot(queries, stacked[0].T, preferred_element_type=jnp.float32) + bias
    )
    sum_ref[...] = (
        lax.broadcasted_iota(jnp.int32, (tile_queries, tile), 1) // KIDS
        == lax.broadcasted_iota(jnp.int32, (tile_queries, tile), 0)
    ).astype(jnp.bfloat16)
    total_ref[...] = jnp.zeros(total_ref.shape, jnp.float32)
    for copy in ahead:
        copy.wait()

    def gather(block, k):
        for i in range(tile_queries):
            for t in range(SLOT):
                at = pl.multiple_of(place_ref[block, t, k * tile_queries + i], 2)
                found_ref[k, pl.ds(i * KIDS + 2 * t, 2), :] = table_ref[pl.ds(at, 2), :]

    def queries_of(j, k):
        if isinstance(j, int):
            return slice(j * rows + k * tile_queries, j * rows + (k + 1) * tile_queries)
        return pl.ds(pl.multiple_of(j * rows + k * tile_queries, SUBLANES), tile_queries)

    def score(j, k):
        some = queries_of(j, k)
        nodes = found_ref[k]
        spread = jnp.broadcast_to(query_ref[some, :][:, None, :], (tile_queries, KIDS, feat))
        crossed = (nodes * spread.reshape(tile, feat)).astype(jnp.bfloat16)
        joined = jnp.concatenate([nodes.astype(jnp.bfloat16), crossed], axis=1)
        pre = jnp.dot(joined, mix_ref[...], preferred_element_type=jnp.float32)
        pre = pre.reshape(tile_queries, KIDS, hidden_width) + start_ref[some, :][:, None, :]
        weighed = jnp.maximum(pre.reshape(tile, hidden_width), 0.0) * out_row_ref[0:1, :]
        return jnp.sum(weighed, axis=1, keepdims=True)

    def settle(j, c, k, scores):
        some = queries_of(j, k)
        need = need_ref[some, :]
        if isinstance(c, int):
            need = need[:, c * SLOT : (c + 1) * SLOT]
        else:
            need = pltpu.roll(need, (width - c * SLOT) % width, 1)
        key = key_ref[some, :]
        above = key >> 1
        parity = key & 1
        code = jnp.full((tile_queries, width), -1, jnp.int32)
        for t in range(SLOT):
            code = jnp.where(above == need[:, t : t + 1], 2 * t + parity, code)
        slot = lax.broadcasted_iota(jnp.int32, (tile_queries, KIDS, width), 1)
        hits = jnp.where(code[:, None, :] == slot, scores.reshape(tile_queries, KIDS, 1), 0.0)
        total_ref[some, :] += jnp.dot(
            sum_ref[...],
            hits.reshape(tile, width).astype(jnp.bfloat16),
            preferred_element_type=jnp.float32,
        )

    def one_pass(j, c, block):
        gather(block, 0)
        before = None
        for k in range(tiles):
            if k + 1 < tiles:
                gather(block, k + 1)
            scores = score(j, k)
            if k > 0:
                settle(j, c, k - 1, before)
            before = scores
        settle(j, c, tiles - 1, before)

    def late_pass(j, c):
        copy = pltpu.make_async_copy(
            flat_ref.at[j * limit + c], place_ref.at[turns * READY], done.at[turns]
        )
        copy.start()
        copy.wait()
        one_pass(j, c, turns * READY)

    if turns <= STATIC:
        for j in range(turns):
            for c in range(READY):
                pl.when(passes_ref[j] > c)(functools.partial(one_pass, j, c, j * READY + c))

            def later(c, carry, j=j):
                late_pass(j, c)
                return carry

            lax.fori_loop(READY, passes_ref[j], later, 0)
    else:

        def one_source(j, carry):
            def every(c, inner):
                late_pass(j, c)
                return inner

            return lax.fori_loop(0, passes_ref[j], every, carry)

        lax.fori_loop(0, turns, one_source, 0)
    for j, out_ref in enumerate(outs):
        out_ref[...] = total_ref[j * rows : (j + 1) * rows, :].T.astype(out_ref.dtype)


def score_sources(asked, rows, shard_rows, wide, packs):
    turns = len(asked)
    feat = asked[0].shape[1]
    width = feat
    digits = asked[0].shape[0] // rows - 1
    part = (packs[0].shape[0] - 16) // 3
    hidden = part * len(packs)
    tile_queries = next(n for n in (48, 32, 24, 16, 8) if rows % n == 0)
    tile = tile_queries * KIDS
    lanes = -(-rows // LANES) * LANES
    count = turns * rows
    return pl.pallas_call(
        functools.partial(score_kernel, shard_rows, digits, turns, len(packs), tile_queries),
        in_specs=[VMEM] * (turns + 1 + len(packs)),
        out_specs=(VMEM,) * turns,
        out_shape=(jax.ShapeDtypeStruct((width, rows), jnp.bfloat16),) * turns,
        scratch_shapes=[
            pltpu.VMEM((2 * feat, hidden), jnp.bfloat16),
            pltpu.VMEM((SUBLANES, hidden), jnp.float32),
            pltpu.VMEM((tile_queries, tile), jnp.bfloat16),
            pltpu.VMEM((count, feat), jnp.float32),
            pltpu.VMEM((count, hidden), jnp.float32),
            pltpu.VMEM((count, width), jnp.int32),
            pltpu.VMEM((count, width), jnp.int32),
            pltpu.VMEM((turns * (width // 2 // SLOT), SLOT, lanes), jnp.int32),
            pltpu.VMEM((count, width), jnp.float32),
            pltpu.VMEM((rows // tile_queries, tile, feat), jnp.float32),
            pltpu.SMEM((turns * READY + 1, SLOT, lanes), jnp.int32),
            pltpu.SMEM((turns,), jnp.int32),
            pltpu.SemaphoreType.DMA((turns + 1,)),
        ],
        compiler_params=pltpu.CompilerParams(vmem_limit_bytes=16 * 2**20),
        cost_estimate=pl.CostEstimate(
            flops=2 * count * KIDS * 3 * feat * hidden,
            bytes_accessed=4 * count * KIDS * feat,
            transcendentals=0,
        ),
    )(*asked, wide, *packs)


def mirrored(value, count):
    result = 0
    while count > 1:
        result = result * 2 + value % 2
        value //= 2
        count //= 2
    return result


def far_first(count):
    return sorted(range(1, count), key=lambda step: (step < 2, step))


def shards(queries, node_table, beam, w_query, w_node, w_cross, bias_hidden, w_out):
    groups = lax.axis_size("blk")
    parts = lax.axis_size("hid")
    rows, width = beam.shape
    shard_rows = node_table.shape[0]
    binary = groups & (groups - 1) == 0 and parts & (parts - 1) == 0
    turns = groups // parts

    def hop_pairs(turn, back):
        pairs = []
        for b in range(groups):
            for h in range(parts):
                k = (mirrored(h, parts) if binary else h) * turns + turn
                if binary:
                    to = b ^ k
                else:
                    to = (b - k) % groups if not back else (b + k) % groups
                pairs.append((b * parts + h, to * parts + h))
        return pairs

    def hop(value, turn, back=False):
        return lax.ppermute(value, ("blk", "hid"), hop_pairs(turn, back))

    def across(value, step):
        pairs = [(h, h ^ step if binary else (h + step) % parts) for h in range(parts)]
        return lax.ppermute(value, "hid", pairs)

    digits = -(-(groups * shard_rows - 1).bit_length() // SHIFT)
    message, weights = pack(queries, beam, digits, (w_query, w_node, w_cross), w_out, bias_hidden)
    asked = []
    for turn in range(turns):
        asked.append(hop(message, turn))
    packs = [weights]
    for step in far_first(parts):
        packs.append(across(weights, step))
    scored = score_sources(asked, rows, shard_rows, widen(node_table), packs)
    total = sum(hop(s, turn, True).astype(jnp.float32) for turn, s in enumerate(scored))

    own = lax.axis_index("hid")
    piece = width // parts
    result = lax.dynamic_slice_in_dim(total, own * piece, piece, axis=0)
    for step in far_first(parts):
        peer = own ^ step if binary else (own + step) % parts
        sent = lax.dynamic_slice_in_dim(total, peer * piece, piece, axis=0)
        result = result + across(sent.astype(jnp.bfloat16), step).astype(jnp.float32)
    return result.T


def solution(mesh):
    in_specs = (
        P("blk", None),
        P("blk", None),
        P("blk", None),
        P(None, "hid"),
        P(None, "hid"),
        P(None, "hid"),
        P("hid"),
        P("hid"),
    )
    out_specs = P("blk", "hid")
    return jax.shard_map(shards, mesh=mesh, in_specs=in_specs, out_specs=out_specs, check_vma=False)
```

```python
import functools

import jax
import jax.numpy as jnp
from jax import lax
from jax.experimental import pallas as pl
from jax.experimental.pallas import tpu as pltpu
from jax.sharding import PartitionSpec as P


SLOT = 8
KIDS = 2 * SLOT
READY = 2
FIELD = 20
SHIFT = 16
BIAS = 127
FRACTION = 7
SIGN = 15
LANES = 128
SUBLANES = 8
STATIC = 2

VMEM = pl.BlockSpec(memory_space=pltpu.VMEM)


def code_of(value):
    size = jnp.abs(value)
    kept = size >= 2.0 ** (1 - BIAS)
    exponent = jnp.full(value.shape, BIAS, jnp.int32)
    for k in (64, 32, 16, 8, 4, 2, 1):
        low = size < 2.0 ** (1 - k)
        size = jnp.where(low, size * 2.0**k, size)
        exponent = jnp.where(low, exponent - k, exponent)
    for k in (4, 2, 1):
        high = size >= 2.0**k
        size = jnp.where(high, size * 2.0**-k, size)
        exponent = jnp.where(high, exponent + k, exponent)
    fraction = ((size - 1.0) * 2.0**FRACTION).astype(jnp.int32)
    code = (exponent << FRACTION) + fraction + jnp.where(value < 0, 1 << SIGN, 0)
    return jnp.where(kept, code, 0)


def value_of(code):
    down = BIAS + FRACTION - ((code >> FRACTION) & (2 ** (SIGN - FRACTION) - 1))
    value = ((code & (2**FRACTION - 1)) + 2**FRACTION).astype(jnp.float32)
    for k in (64, 64, 32, 16, 8, 4, 2, 1):
        take = down >= k
        value = jnp.where(take, value * 2.0**-k, value)
        down = jnp.where(take, down - k, down)
    value = jnp.where((code >> SIGN) != 0, -value, value)
    return jnp.where(code == 0, 0.0, value)


def pack_kernel(digits, *refs):
    sources, (message_ref, pack_ref), held, done = refs[:7], refs[7:9], refs[9:-1], refs[-1]
    copies = [
        pltpu.make_async_copy(source, target, done.at[i])
        for i, (source, target) in enumerate(zip(sources, held))
    ]
    for copy in copies:
        copy.start()
    beam_ref, query_ref = held[:2]
    weights, (out_row, bias_row) = held[2:5], held[5:7]
    rows = beam_ref.shape[0]
    part = weights[0].shape[0]
    width = pack_ref.shape[1]
    for copy in copies:
        copy.wait()
    ids = beam_ref[...]
    for d in range(digits):
        digit = (ids >> (SHIFT * (digits - 1 - d))) & (2**SHIFT - 1)
        message_ref[(d + 1) * rows : (d + 2) * rows, :] = digit.astype(jnp.uint16)
    message_ref[0:rows, :] = code_of(query_ref[...].astype(jnp.float32)).astype(jnp.uint16)
    for i, weight in enumerate(weights):
        pack_ref[i * part : (i + 1) * part, :] = weight[...]
    tail = pack_ref.shape[0] - 3 * part
    ends = jnp.concatenate(
        [
            out_row[...].astype(jnp.float32),
            bias_row[...].astype(jnp.float32),
            jnp.zeros((tail - 2, part), jnp.float32),
        ],
        axis=0,
    )
    ends = jnp.concatenate([ends, jnp.zeros((tail, width - part), jnp.float32)], axis=1)
    pack_ref[3 * part :, :] = ends.astype(jnp.bfloat16)


def pack(queries, beam, digits, weights, w_out, bias):
    rows, width = queries.shape
    part = w_out.shape[0]
    given = (beam, queries, *[w.T for w in weights], w_out[None, :], bias[None, :])
    return pl.pallas_call(
        functools.partial(pack_kernel, digits),
        in_specs=[pl.BlockSpec(memory_space=pltpu.HBM)] * len(given),
        out_specs=(VMEM, VMEM),
        out_shape=(
            jax.ShapeDtypeStruct(((digits + 1) * rows, width), jnp.uint16),
            jax.ShapeDtypeStruct((3 * part + 16, width), jnp.bfloat16),
        ),
        scratch_shapes=[pltpu.VMEM(x.shape, x.dtype) for x in given]
        + [pltpu.SemaphoreType.DMA((len(given),))],
        compiler_params=pltpu.CompilerParams(vmem_limit_bytes=60 * 2**20),
    )(*given)


def widen_kernel(chunks, table_ref, wide_ref, held_ref, done):
    rows = table_ref.shape[0] // chunks
    copies = [
        pltpu.make_async_copy(
            table_ref.at[pl.ds(i * rows, rows)], held_ref.at[pl.ds(i * rows, rows)], done.at[i]
        )
        for i in range(chunks)
    ]
    for copy in copies:
        copy.start()
    for i, copy in enumerate(copies):
        copy.wait()
        some = slice(i * rows, (i + 1) * rows)
        wide_ref[some, :] = held_ref[some, :].astype(jnp.float32)


def widen(table):
    rows, width = table.shape
    chunks = 8
    return pl.pallas_call(
        functools.partial(widen_kernel, chunks),
        in_specs=[pl.BlockSpec(memory_space=pltpu.HBM)],
        out_specs=VMEM,
        out_shape=jax.ShapeDtypeStruct((rows, width), jnp.float32),
        scratch_shapes=[pltpu.VMEM((rows, width), table.dtype), pltpu.SemaphoreType.DMA((chunks,))],
        compiler_params=pltpu.CompilerParams(vmem_limit_bytes=12 * 2**20),
        cost_estimate=pl.CostEstimate(flops=0, bytes_accessed=6 * rows * width, transcendentals=0),
    )(table)


def score_kernel(shard_rows, digits, turns, parts, tile_queries, *refs):
    asked, table_ref, packs = refs[:turns], refs[turns], refs[turns + 1 : turns + 1 + parts]
    outs = refs[turns + 1 + parts : 2 * turns + 1 + parts]
    (
        mix_ref,
        out_row_ref,
        sum_ref,
        query_ref,
        start_ref,
        key_ref,
        need_ref,
        flat_ref,
        total_ref,
        found_ref,
        place_ref,
        passes_ref,
        done,
    ) = refs[2 * turns + 1 + parts :]
    width, rows = outs[0].shape
    feat = table_ref.shape[1]
    hidden_width = mix_ref.shape[1]
    part = hidden_width // parts
    tile = tile_queries * KIDS
    tiles = rows // tile_queries
    limit = width // 2 // SLOT

    ids = jnp.concatenate([a[rows : 2 * rows, :].astype(jnp.int32) for a in asked], axis=0)
    for d in range(2, digits + 1):
        digit = [a[d * rows : (d + 1) * rows, :].astype(jnp.int32) for a in asked]
        ids = (ids << SHIFT) + jnp.concatenate(digit, axis=0)
    local = ids - lax.axis_index("blk") * shard_rows
    owned = (local >= 0) & (local < shard_rows)
    even = owned & ((local & 1) == 0)
    lane = lax.broadcasted_iota(jnp.int32, (turns * rows, width), 1)
    earlier = (
        lax.broadcasted_iota(jnp.int32, (width, width), 0)
        < lax.broadcasted_iota(jnp.int32, (width, width), 1)
    ).astype(jnp.bfloat16)
    even_count = even.astype(jnp.float32)
    rank = jnp.dot(even_count.astype(jnp.bfloat16), earlier, preferred_element_type=jnp.float32)
    shift = lane - rank.astype(jnp.int32)
    word = jnp.where(even, (local >> 1) + (shift << FIELD) + (1 << (FIELD + 8)), 0)
    hop = 1
    while hop < width:
        bit = hop << FIELD
        moved = pltpu.roll(word, width - hop, 1)
        word = jnp.where((moved & bit) != 0, moved, jnp.where((word & bit) != 0, 0, word))
        hop *= 2
    front = word & ((1 << FIELD) - 1)
    ahead = []
    for j in range(turns):
        slots = (front[j * rows : (j + 1) * rows, :] * 2).T
        for c in range(limit):
            flat_ref[j * limit + c, :, 0:rows] = slots[c * SLOT : (c + 1) * SLOT, :]
        ahead.append(
            pltpu.make_async_copy(
                flat_ref.at[pl.ds(j * limit, READY)],
                place_ref.at[pl.ds(j * READY, READY)],
                done.at[j],
            )
        )
        ahead[-1].start()
        most = jnp.max(
            jnp.sum(even_count[j * rows : (j + 1) * rows, :], axis=1, keepdims=True)
        ).astype(jnp.int32)
        passes_ref[j] = (most + (SLOT - 1)) // SLOT
    need_ref[...] = jnp.where(word != 0, front, -1)
    key_ref[...] = jnp.where(owned, local, -4)

    stacked = [
        jnp.concatenate([p[i * part : (i + 1) * part, :] for p in packs], axis=0) for i in range(3)
    ]
    mix_ref[0:feat, :] = stacked[1].T
    mix_ref[feat:, :] = stacked[2].T
    ends = [p[3 * part :, :].astype(jnp.float32) for p in packs]
    out_row = jnp.concatenate([e[0:1, 0:part] for e in ends], axis=1)
    bias = jnp.concatenate([e[1:2, 0:part] for e in ends], axis=1)
    out_row_ref[...] = jnp.broadcast_to(out_row, out_row_ref.shape)
    codes = jnp.concatenate([a[0:rows, :].astype(jnp.int32) for a in asked], axis=0)
    exact = value_of(codes)
    query_ref[...] = exact
    queries = exact.astype(jnp.bfloat16)
    start_ref[...] = (
        jnp.dot(queries, stacked[0].T, preferred_element_type=jnp.float32) + bias
    )
    sum_ref[...] = (
        lax.broadcasted_iota(jnp.int32, (tile_queries, tile), 1) // KIDS
        == lax.broadcasted_iota(jnp.int32, (tile_queries, tile), 0)
    ).astype(jnp.bfloat16)
    total_ref[...] = jnp.zeros(total_ref.shape, jnp.float32)
    for copy in ahead:
        copy.wait()

    def gather(block, k):
        for i in range(tile_queries):
            for t in range(SLOT):
                at = pl.multiple_of(place_ref[block, t, k * tile_queries + i], 2)
                found_ref[k, pl.ds(i * KIDS + 2 * t, 2), :] = table_ref[pl.ds(at, 2), :]

    def queries_of(j, k):
        if isinstance(j, int):
            return slice(j * rows + k * tile_queries, j * rows + (k + 1) * tile_queries)
        return pl.ds(pl.multiple_of(j * rows + k * tile_queries, SUBLANES), tile_queries)

    def score(j, k):
        some = queries_of(j, k)
        nodes = found_ref[k]
        spread = jnp.broadcast_to(query_ref[some, :][:, None, :], (tile_queries, KIDS, feat))
        crossed = (nodes * spread.reshape(tile, feat)).astype(jnp.bfloat16)
        joined = jnp.concatenate([nodes.astype(jnp.bfloat16), crossed], axis=1)
        pre = jnp.dot(joined, mix_ref[...], preferred_element_type=jnp.float32)
        pre = pre.reshape(tile_queries, KIDS, hidden_width) + start_ref[some, :][:, None, :]
        weighed = jnp.maximum(pre.reshape(tile, hidden_width), 0.0) * out_row_ref[0:1, :]
        return jnp.sum(weighed, axis=1, keepdims=True)

    def settle(j, c, k, scores):
        some = queries_of(j, k)
        need = need_ref[some, :]
        if isinstance(c, int):
            need = need[:, c * SLOT : (c + 1) * SLOT]
        else:
            need = pltpu.roll(need, (width - c * SLOT) % width, 1)
        key = key_ref[some, :]
        above = key >> 1
        parity = key & 1
        code = jnp.full((tile_queries, width), -1, jnp.int32)
        for t in range(SLOT):
            code = jnp.where(above == need[:, t : t + 1], 2 * t + parity, code)
        slot = lax.broadcasted_iota(jnp.int32, (tile_queries, KIDS, width), 1)
        hits = jnp.where(code[:, None, :] == slot, scores.reshape(tile_queries, KIDS, 1), 0.0)
        total_ref[some, :] += jnp.dot(
            sum_ref[...],
            hits.reshape(tile, width).astype(jnp.bfloat16),
            preferred_element_type=jnp.float32,
        )

    def one_pass(j, c, block):
        gather(block, 0)
        before = None
        for k in range(tiles):
            if k + 1 < tiles:
                gather(block, k + 1)
            scores = score(j, k)
            if k > 0:
                settle(j, c, k - 1, before)
            before = scores
        settle(j, c, tiles - 1, before)

    def late_pass(j, c):
        copy = pltpu.make_async_copy(
            flat_ref.at[j * limit + c], place_ref.at[turns * READY], done.at[turns]
        )
        copy.start()
        copy.wait()
        one_pass(j, c, turns * READY)

    if turns <= STATIC:
        for j in range(turns):
            for c in range(READY):
                pl.when(passes_ref[j] > c)(functools.partial(one_pass, j, c, j * READY + c))

            def later(c, carry, j=j):
                late_pass(j, c)
                return carry

            lax.fori_loop(READY, passes_ref[j], later, 0)
    else:

        def one_source(j, carry):
            def every(c, inner):
                late_pass(j, c)
                return inner

            return lax.fori_loop(0, passes_ref[j], every, carry)

        lax.fori_loop(0, turns, one_source, 0)
    for j, out_ref in enumerate(outs):
        out_ref[...] = total_ref[j * rows : (j + 1) * rows, :].T.astype(out_ref.dtype)


def score_sources(asked, rows, shard_rows, wide, packs):
    turns = len(asked)
    feat = asked[0].shape[1]
    width = feat
    digits = asked[0].shape[0] // rows - 1
    part = (packs[0].shape[0] - 16) // 3
    hidden = part * len(packs)
    tile_queries = next(n for n in (48, 32, 24, 16, 8) if rows % n == 0)
    tile = tile_queries * KIDS
    lanes = -(-rows // LANES) * LANES
    count = turns * rows
    return pl.pallas_call(
        functools.partial(score_kernel, shard_rows, digits, turns, len(packs), tile_queries),
        in_specs=[VMEM] * (turns + 1 + len(packs)),
        out_specs=(VMEM,) * turns,
        out_shape=(jax.ShapeDtypeStruct((width, rows), jnp.bfloat16),) * turns,
        scratch_shapes=[
            pltpu.VMEM((2 * feat, hidden), jnp.bfloat16),
            pltpu.VMEM((SUBLANES, hidden), jnp.float32),
            pltpu.VMEM((tile_queries, tile), jnp.bfloat16),
            pltpu.VMEM((count, feat), jnp.float32),
            pltpu.VMEM((count, hidden), jnp.float32),
            pltpu.VMEM((count, width), jnp.int32),
            pltpu.VMEM((count, width), jnp.int32),
            pltpu.VMEM((turns * (width // 2 // SLOT), SLOT, lanes), jnp.int32),
            pltpu.VMEM((count, width), jnp.float32),
            pltpu.VMEM((rows // tile_queries, tile, feat), jnp.float32),
            pltpu.SMEM((turns * READY + 1, SLOT, lanes), jnp.int32),
            pltpu.SMEM((turns,), jnp.int32),
            pltpu.SemaphoreType.DMA((turns + 1,)),
        ],
        compiler_params=pltpu.CompilerParams(vmem_limit_bytes=16 * 2**20),
        cost_estimate=pl.CostEstimate(
            flops=2 * count * KIDS * 3 * feat * hidden,
            bytes_accessed=4 * count * KIDS * feat,
            transcendentals=0,
        ),
    )(*asked, wide, *packs)


def mirrored(value, count):
    result = 0
    while count > 1:
        result = result * 2 + value % 2
        value //= 2
        count //= 2
    return result


def far_first(count):
    return sorted(range(1, count), key=lambda step: (step < 2, step))


def shards(queries, node_table, beam, w_query, w_node, w_cross, bias_hidden, w_out):
    groups = lax.axis_size("blk")
    parts = lax.axis_size("hid")
    rows, width = beam.shape
    shard_rows = node_table.shape[0]
    binary = groups & (groups - 1) == 0 and parts & (parts - 1) == 0
    turns = groups // parts

    def hop_pairs(turn, back):
        pairs = []
        for b in range(groups):
            for h in range(parts):
                k = (mirrored(h, parts) if binary else h) * turns + turn
                if binary:
                    to = b ^ k
                else:
                    to = (b - k) % groups if not back else (b + k) % groups
                pairs.append((b * parts + h, to * parts + h))
        return pairs

    def hop(value, turn, back=False):
        return lax.ppermute(value, ("blk", "hid"), hop_pairs(turn, back))

    def across(value, step):
        pairs = [(h, h ^ step if binary else (h + step) % parts) for h in range(parts)]
        return lax.ppermute(value, "hid", pairs)

    digits = -(-(groups * shard_rows - 1).bit_length() // SHIFT)
    message, weights = pack(queries, beam, digits, (w_query, w_node, w_cross), w_out, bias_hidden)
    asked = []
    for turn in range(turns):
        asked.append(hop(message, turn))
    packs = [weights]
    for step in far_first(parts):
        packs.append(across(weights, step))
    scored = score_sources(asked, rows, shard_rows, widen(node_table), packs)
    total = sum(hop(s, turn, True).astype(jnp.float32) for turn, s in enumerate(scored))

    own = lax.axis_index("hid")
    piece = width // parts
    result = lax.dynamic_slice_in_dim(total, own * piece, piece, axis=0)
    for step in far_first(parts):
        peer = own ^ step if binary else (own + step) % parts
        sent = lax.dynamic_slice_in_dim(total, peer * piece, piece, axis=0)
        result = result + across(sent.astype(jnp.bfloat16), step).astype(jnp.float32)
    return result.T


def solution(mesh):
    in_specs = (
        P("blk", None),
        P("blk", None),
        P("blk", None),
        P(None, "hid"),
        P(None, "hid"),
        P(None, "hid"),
        P("hid"),
        P("hid"),
    )
    out_specs = P("blk", "hid")
    return jax.shard_map(shards, mesh=mesh, in_specs=in_specs, out_specs=out_specs, check_vma=False)
```
